32 devices in a mesh: space: 8 (over z, x), section: 2 (over core), dp: 2 (over y).
Axes of the slice: x: 2, y: 2, z: 4, core: 2. Of those that a mesh axis runs over, the one named last changes fastest.
Arguments:
- input_field: bfloat16 [2, 2, 16, 8, 8, 256], P(None, 'dp', 'space'), may hold values from -6 to 6
- first_weight: bfloat16 [864, 64], replicated, may hold values from -0.21875 to 0.21875
- second_weight: bfloat16 [1728, 128], replicated, may hold values from -0.15625 to 0.15625
- upstream_grad: bfloat16 [2, 2, 4, 8, 2, 256], P(None, 'dp', None, 'space'), may hold values from -0.25 to 0.25
Outputs:
- first_weight_grad: float32 [864, 64], P('space', 'section')
- second_weight_grad: float32 [1728, 128], P('space', 'section')
The draws below stay inside these ranges and needn't reach their ends.
All inputs are finite; a program needn't handle non-finite values.
Results may differ from the reference program's by a relative error of at most 0.023.
Values may be sent and summed in bfloat16 or wider, within the bound.
No kernel may reach another device: no remote copies, remote signals or barrier semaphores. Data moves between devices by JAX's collectives and lax.ppermute only.
A program may use at most 64 MiB of HBM per device.

```python
import jax
import jax.numpy as jnp
from jax import lax

CA = 32
CB = 64
CC = 128
TAPS = 27
YS = 8
ZS = 8
MICRO = 2
VOLUMES = 8
REPLICAS = 2
XS = 16
XB = 4
YB = 2
ZB = 2


def levels(own_key, extent, cuts, low, high):
    def one(dim, shards_of):
        draws = jax.random.uniform(jax.random.fold_in(jax.random.fold_in(own_key, 6), dim), (shards_of,), jnp.float32, low / len(cuts), high / len(cuts))
        return jnp.repeat(jnp.exp(draws), extent[dim] // shards_of).reshape((-1,) + (1,) * (len(extent) - dim - 1))

    gain = one(*cuts[0])
    for cut in cuts[1:]:
        gain = gain * one(*cut)
    return gain


def noise(key, extent, width, reach, split=(), held_as=jnp.bfloat16):
    drawn = jax.random.normal(key, extent, jnp.float32) * width
    if len(split) > 0:
        drawn = levels(key, extent, split, -0.22, 0.18) * drawn
    return jnp.clip(drawn, min=-reach, max=reach).astype(held_as)


def setup_inputs(seed: int = 0) -> dict:
    splits = jax.random.split(jax.random.key(seed), 5)
    return {
        "input_field": noise(splits[0], (MICRO, REPLICAS, XS, VOLUMES, YS, ZS * CA), 1.0, 6.0, ((1, 2), (2, 8))),
        "first_weight": noise(splits[1], (TAPS * CA, CB), (TAPS * CA) ** -0.5, 0.21875),
        "second_weight": noise(splits[2], (TAPS * CB, CC), (TAPS * CB) ** -0.5, 0.15625),
        "upstream_grad": noise(splits[3], (MICRO, REPLICAS, XB, VOLUMES, YB, ZB * CC), (MICRO * REPLICAS * VOLUMES * XB * YB * ZB) ** -0.5, 0.25, ((1, 2), (3, 8))),
    }


SLOPE = 0.3

def split_three(volume, position, front_plane):
    half_count = volume.shape[position] // 2
    paired = volume.reshape(volume.shape[:position] + (half_count, 2) + volume.shape[position + 1:])
    even_cells = lax.index_in_dim(paired, 0, position + 1, keepdims=False)
    odd_cells = lax.index_in_dim(paired, 1, position + 1, keepdims=False)
    earlier = jnp.concatenate([front_plane, lax.slice_in_dim(odd_cells, 0, half_count - 1, axis=position)], axis=position)
    return [earlier, even_cells, odd_cells]

def edge_zeros(volume, position):
    target_shape = volume.shape[:position] + (1,) + volume.shape[position + 1:]
    return jnp.zeros(target_shape, volume.dtype)

def patches(volume, front_plane):
    pieces = []
    for along_x in split_three(volume, 0, front_plane):
        for along_y in split_three(along_x, 2, edge_zeros(along_x, 2)):
            for along_z in split_three(along_y, 3, edge_zeros(along_y, 3)):
                pieces.append(along_z)
    return jnp.concatenate(pieces, axis=-1)

def scatter_back(column_grad, target_shape):
    zero_field = jnp.zeros(target_shape, jnp.float32)
    front_plane = jnp.zeros((1,) + tuple(target_shape[1:]), jnp.float32)
    result, pullback = jax.vjp(lambda volume: patches(volume, front_plane), zero_field)
    return pullback(column_grad)[0]

def first_grad(columns, hidden, arrived):
    grad_rows = arrived.reshape(-1, CB).astype(jnp.float32)
    delta_rows = jnp.where(hidden.reshape(-1, CB) > 0, grad_rows, SLOPE * grad_rows).astype(jnp.bfloat16)
    return lax.dot_general(columns, delta_rows, (((0,), (0,)), ((), ())), preferred_element_type=jnp.float32)

def second_step(arrived, grad_out, second_weight):
    planes, local_count, rows_y, packed = arrived.shape
    cells_z = packed // CB
    volume = arrived.reshape(planes, local_count, rows_y, cells_z, CB)
    front_plane = jnp.zeros((1, local_count, rows_y, cells_z, CB), arrived.dtype)
    columns = patches(volume, front_plane).reshape(-1, TAPS * CB)
    preact = jnp.dot(columns, second_weight, preferred_element_type=jnp.float32)
    grad_rows = grad_out.reshape(-1, CC).astype(jnp.float32)
    delta_rows = jnp.where(preact > 0, grad_rows, SLOPE * grad_rows).astype(jnp.bfloat16)
    weight_grad = lax.dot_general(columns, delta_rows, (((0,), (0,)), ((), ())), preferred_element_type=jnp.float32)
    column_grad = lax.dot_general(delta_rows, second_weight, (((1,), (1,)), ((), ())), preferred_element_type=jnp.float32)
    column_grad = column_grad.reshape(planes // 2, local_count, rows_y // 2, cells_z // 2, TAPS * CB)
    back_grad = scatter_back(column_grad, volume.shape).astype(jnp.bfloat16)
    return (weight_grad, back_grad.reshape(arrived.shape))

def reference(input_field, first_weight, second_weight, upstream_grad):
    fields = input_field.reshape((MICRO * REPLICAS,) + input_field.shape[2:])
    grads_out = upstream_grad.reshape((MICRO * REPLICAS,) + upstream_grad.shape[2:])

    def one_round(carried, inputs):
        first_sum, second_sum = carried
        source, grad_out = inputs
        volume = source.reshape(XS, VOLUMES, YS, ZS, CA)
        front_plane = jnp.zeros((1, VOLUMES, YS, ZS, CA), source.dtype)
        columns = patches(volume, front_plane).reshape(-1, TAPS * CA)
        preact = jnp.dot(columns, first_weight, preferred_element_type=jnp.float32)
        hidden = jnp.where(preact > 0, preact, SLOPE * preact).astype(jnp.bfloat16)
        arrived = hidden.reshape(XS // 2, VOLUMES, YS // 2, ZS // 2 * CB)
        weight_grad, back_grad = second_step(arrived, grad_out, second_weight)
        first_new = first_sum + first_grad(columns, hidden, back_grad)
        return ((first_new, second_sum + weight_grad), None)
    start_sums = (jnp.zeros((TAPS * CA, CB), jnp.float32), jnp.zeros((TAPS * CB, CC), jnp.float32))
    carried = lax.scan(one_round, start_sums, (fields, grads_out))[0]
    return (carried[0], carried[1])
```

```python
import jax
import jax.numpy as jnp
from jax import lax
from jax.experimental import pallas as pl
from jax.experimental.pallas import tpu as pltpu
from jax.sharding import PartitionSpec as P

CA = 32
CB = 64
CC = 128
TAPS = 27
SLOPE = 0.3
BF16 = jnp.bfloat16
F32 = jnp.float32


def round_up(value, step):
    return -(-value // step) * step


def leaky(condition, value):
    return jnp.where(condition > 0, value, SLOPE * value)


def contract(a, b, dim_a, dim_b):
    return lax.dot_general(a, b, (((dim_a,), (dim_b,)), ((), ())), preferred_element_type=F32)


def call(body, out_shape, scratch, args):
    vmem = pl.BlockSpec(memory_space=pltpu.VMEM)
    many = isinstance(out_shape, (list, tuple))
    return pl.pallas_call(
        body,
        out_shape=out_shape,
        in_specs=[vmem] * len(args),
        out_specs=[vmem] * len(out_shape) if many else vmem,
        scratch_shapes=scratch,
        compiler_params=pltpu.CompilerParams(vmem_limit_bytes=48 << 20),
    )(*args)


def banded_body(weight, banded):
    lane = lax.broadcasted_iota(jnp.int32, (CA, 2 * CB), 1)
    zero = jnp.zeros((CA, 2 * CB), F32)
    for tap in range(9):
        left, right = [], []
        for kz in range(3):
            part = weight[pl.ds((3 * tap + kz) * CA, CA), :].astype(F32)
            both = jnp.concatenate([part, part], axis=1)
            left.append(jnp.where(lane < CB, both, 0.0))
            right.append(jnp.where(lane < CB, 0.0, both))
        for half in range(2):
            rows = []
            for z in range(8):
                block = zero
                for odd, side in ((0, left), (1, right)):
                    kz = z - 2 * (2 * half + odd) + 1
                    if 0 <= kz <= 2:
                        block = block + side[kz]
                rows.append(block)
            banded[pl.ds(tap * 256, 256), half * 128 : half * 128 + 128] = jnp.concatenate(
                rows, axis=0
            ).astype(BF16)


def main_body(count, spread, mine, got, before, upstream, banded, second, keep, send, xf, hid, hgs, t2, t1):
    side = lax.axis_index("space") % 2
    section = lax.axis_index("section")
    rows = count * 4
    planes = [before[i] for i in range(3)]
    own, other = [mine[0], mine[1]], [got[0], got[1]]
    first = side == 0
    planes += [jnp.where(first, own[i], other[i]) for i in range(2)]
    planes += [jnp.where(first, other[i], own[i]) for i in range(2)]
    row = lax.broadcasted_iota(jnp.int32, (rows, 256), 0)
    tiles = []
    for i, plane in enumerate(planes):
        flat = plane.reshape(count * 8, 256).astype(F32)
        for h in range(2):
            xf[i, h, 0:8, :] = jnp.zeros((8, 128), F32)
            xf[i, h, pl.ds(8, count * 8), :] = flat[:, h * 128 : h * 128 + 128]
        triple = []
        for ky in range(3):
            part = jnp.concatenate(
                [xf[i, h, pl.ds(7 + ky, rows, stride=2), :] for h in range(2)], axis=1
            )
            if ky == 0:
                part = jnp.where(row % 4 == 0, 0.0, part)
            triple.append(part.astype(BF16))
        tiles.append(triple)
    columns = [
        jnp.concatenate([tiles[2 * i + kx][ky] for i in range(3)], axis=0)
        for kx in range(3)
        for ky in range(3)
    ]
    preact = jnp.dot(jnp.concatenate(columns, axis=1), banded[...], preferred_element_type=F32)
    hidden = leaky(preact, preact).astype(BF16).astype(F32)
    half = count * 2
    lane = lax.broadcasted_iota(jnp.int32, (half, 128), 1)
    low = lane < CB
    row2 = lax.broadcasted_iota(jnp.int32, (half, 128), 0)
    cols = []
    for kx in range(3):
        for h in range(2):
            hid[kx, h, 0:8, :] = jnp.zeros((8, 128), F32)
            hid[kx, h, pl.ds(8, rows), :] = hidden[
                kx * rows : kx * rows + rows, h * 128 : h * 128 + 128
            ]
        for ky in range(3):
            a = hid[kx, 0, pl.ds(7 + ky, half, stride=2), :]
            b = hid[kx, 1, pl.ds(7 + ky, half, stride=2), :]
            if ky == 0:
                a = jnp.where(row2 % 2 == 0, 0.0, a)
                b = jnp.where(row2 % 2 == 0, 0.0, b)
            ra = pltpu.roll(a, 64, 1)
            rb = pltpu.roll(b, 64, 1)
            zero_k = jnp.concatenate([jnp.where(low, 0.0, ra), ra[:, :CB]], axis=1)
            one_k = jnp.concatenate([jnp.where(low, ra, rb), rb[:, :CB]], axis=1)
            cols.append(jnp.concatenate([zero_k, one_k], axis=0).astype(BF16))
    out = jnp.zeros((2 * half, CC), F32)
    for tap in range(9):
        out = out + jnp.dot(
            cols[tap], second[pl.ds(tap * 192, 192), :], preferred_element_type=F32
        )
    up = upstream[...].reshape(half, 256).astype(F32)
    up = jnp.concatenate([up[:, :128], up[:, 128:]], axis=0)
    delta = leaky(out, up)
    delta_b = delta.astype(BF16)
    turned = jnp.where(section == 0, delta, pltpu.roll(delta, 64, 1)).astype(BF16)
    for tap in range(9):
        t2[pl.ds(tap * 192, 192), :] = contract(cols[tap], turned, 0, 0)
    row3 = lax.broadcasted_iota(jnp.int32, (2 * half, 128), 0)
    for kx in range(3):
        parts = []
        for ky in range(3):
            base = (3 * kx + ky) * 192
            c0 = contract(delta_b, second[pl.ds(base, 128), :], 1, 1)
            c1 = contract(delta_b, second[pl.ds(base + 128, 64), :], 1, 1)
            parts.append((c0, jnp.concatenate([c1, c1], axis=1)))
        odd = []
        for late, early in zip(parts[2], parts[0]):
            shifted = pltpu.roll(early, 2 * half - 1, 0)
            odd.append(late + jnp.where(row3 % 2 == 0, shifted, 0.0))
        for parity, (c0, c1) in enumerate((parts[1], odd)):
            turn = pltpu.roll(c0, 64, 1)
            k0, k1 = turn[:half], turn[half:]
            a = jnp.where(low, k0, c1[:half] + k1)
            b = jnp.where(low, k1, c1[half:])
            hgs[kx, 0, pl.ds(parity, half, stride=2), :] = a
            hgs[kx, 1, pl.ds(parity, half, stride=2), :] = b
    hidden_grad = jnp.concatenate(
        [jnp.concatenate([hgs[kx, h] for kx in range(3)], axis=0) for h in range(2)], axis=1
    )
    hidden_grad = hidden_grad.astype(BF16).astype(F32)
    delta_a = leaky(hidden, hidden_grad).astype(BF16)
    wide = lax.broadcasted_iota(jnp.int32, (96, 128), 1) < CB
    for tap in range(9):
        grid = contract(columns[tap], delta_a, 0, 0)
        g0, g1 = grid[:, :128], grid[:, 128:]
        left = jnp.concatenate([g1[96:128], g0[0:64] + g1[128:192]], axis=0)
        right = g0[32:128] + g1[160:256]
        fold = jnp.where(wide, left, right)
        fold = fold + pltpu.roll(fold, 64, 1)
        t1[pl.ds(tap * 96, 96), :] = jnp.where(section == 0, fold, pltpu.roll(fold, 32, 1))
    r2, r1 = TAPS * CB // spread, TAPS * CA // spread
    h2, h1 = packed_rows(spread)
    t2[pl.ds(TAPS * CB, t2.shape[0] - TAPS * CB), :] = jnp.zeros((t2.shape[0] - TAPS * CB, 128), F32)
    t1[pl.ds(TAPS * CA, t1.shape[0] - TAPS * CA), :] = jnp.zeros((t1.shape[0] - TAPS * CA, 128), F32)
    low2 = lax.broadcasted_iota(jnp.int32, (h2, 128), 1) < CB
    quarter = lax.broadcasted_iota(jnp.int32, (h1, 128), 1) // 32
    for d in range(spread):
        a = t2[pl.ds(d * r2, h2), :]
        b = t2[pl.ds(d * r2 + h2, h2), :]
        keep[d, 0:h2, :] = jnp.where(low2, a, pltpu.roll(b, 64, 1)).astype(BF16)
        send[d, 0:h2, :] = jnp.where(low2, pltpu.roll(a, 64, 1), b).astype(BF16)
        kept, sent = None, None
        for g in range(4):
            straight = t1[pl.ds(d * r1 + g * h1, h1), :]
            turn = pltpu.roll(straight, 32, 1)
            k, o = (straight, turn) if g % 2 == 0 else (turn, straight)
            kept = k if g == 0 else jnp.where(quarter == g, k, kept)
            sent = o if g == 0 else jnp.where(quarter == g, o, sent)
        keep[d, h2 : h2 + h1, :] = kept.astype(BF16)
        send[d, h2 : h2 + h1, :] = sent.astype(BF16)


def packed_rows(spread):
    r2, r1 = TAPS * CB // spread, TAPS * CA // spread
    return round_up(-(-r2 // 2), 16), round_up(-(-r1 // 4), 16)


def unpack_body(spread, mine, got, first_out, second_out):
    r2, r1 = TAPS * CB // spread, TAPS * CA // spread
    h2, h1 = packed_rows(spread)
    total = mine[...].astype(F32) + got[...].astype(F32)
    top, rest = total[:h2], total[h2:]
    second_out[0:h2, :] = top[:, :CB]
    second_out[pl.ds(h2, r2 - h2), :] = pltpu.roll(top, 64, 1)[: r2 - h2, :CB]
    for g in range(4):
        size = min(h1, r1 - g * h1)
        if size > 0:
            part = rest if g == 0 else pltpu.roll(rest, 128 - 32 * g, 1)
            first_out[pl.ds(g * h1, size), :] = part[:size, : CB // 2]


def swap_bit(count, bit):
    return [(i, i ^ (1 << bit)) for i in range(count)]


def pick(array, index, axis):
    return lax.dynamic_index_in_dim(array, index, axis, keepdims=False)


def shards(input_field, first_weight, second_weight, upstream_grad):
    micro_count, _, planes, volumes, rows_y, packed = input_field.shape
    spread = lax.axis_size("space")
    count = volumes // 2
    pairs = spread // 2
    space = lax.axis_index("space")
    section = lax.axis_index("section")
    side, pair = space % 2, space // 2

    own = pick(input_field[:, 0], section, 0).reshape(planes, count, 2, rows_y, packed)
    mine = pick(own, side, 2)
    got = lax.ppermute(pick(own, 1 - side, 2), "space", swap_bit(spread, 0))
    onward = jnp.where(
        side == 0,
        jnp.stack([mine[1], got[0], got[1]]),
        jnp.stack([got[1], mine[0], mine[1]]),
    )
    before = lax.ppermute(onward, "space", [(i, i + 2) for i in range(spread - 2)])

    up = pick(upstream_grad[:, 0], section, 0)
    bit = 0
    while 1 << bit < pairs:
        up = up.reshape(up.shape[0] // 2, 2, -1, *up.shape[-2:])
        here = (pair >> bit) & 1
        kept = pick(up, here, 1)
        came = lax.ppermute(pick(up, 1 - here, 1), "space", swap_bit(spread, bit + 1))
        up = jnp.where(here == 0, jnp.stack([kept, came], 1), jnp.stack([came, kept], 1))
        up = up.reshape(up.shape[0], -1, *up.shape[-2:])
        bit += 1
    up = up.reshape(count, *up.shape[-2:])

    banded = call(banded_body, jax.ShapeDtypeStruct((9 * 256, 256), BF16), [], (first_weight,))
    h2, h1 = packed_rows(spread)
    block = jax.ShapeDtypeStruct((spread, h2 + h1, 128), BF16)
    kept, outgoing = call(
        lambda *refs: main_body(count, spread, *refs),
        [block, block],
        [
            pltpu.VMEM((7, 2, count * 8 + 16, 128), F32),
            pltpu.VMEM((3, 2, count * 4 + 16, 128), F32),
            pltpu.VMEM((3, 2, count * 4, 128), F32),
            pltpu.VMEM((TAPS * CB + 2 * h2, 128), F32),
            pltpu.VMEM((TAPS * CA + 4 * h1, 128), F32),
        ],
        (mine, got, before, up, banded, second_weight),
    )

    def added(a, b):
        return (a.astype(F32) + b.astype(F32)).astype(BF16)

    total = added(kept, lax.ppermute(outgoing, "section", swap_bit(2, 0)))
    bits = spread.bit_length() - 1
    for bit in range(bits):
        paired = total.reshape(total.shape[0] // 2, 2, *total.shape[1:])
        here = (space >> bit) & 1
        kept = pick(paired, here, 1)
        total = added(kept, lax.ppermute(pick(paired, 1 - here, 1), "space", swap_bit(spread, bit)))
    total = total[0]
    replicas = lax.axis_size("dp")
    bit = 0
    while 1 << (bit + 1) < replicas:
        total = added(total, lax.ppermute(total, "dp", swap_bit(replicas, bit)))
        bit += 1
    came = lax.ppermute(total, "dp", swap_bit(replicas, bit))
    return tuple(
        call(
            lambda *refs: unpack_body(spread, *refs),
            [
                jax.ShapeDtypeStruct((TAPS * CA // spread, CB // 2), F32),
                jax.ShapeDtypeStruct((TAPS * CB // spread, CC // 2), F32),
            ],
            [],
            (total, came),
        )
    )


def solution(mesh):
    return jax.shard_map(
        shards,
        mesh=mesh,
        in_specs=(
            P(None, "dp", "space", None, None, None),
            P(),
            P(),
            P(None, "dp", None, "space", None, None),
        ),
        out_specs=(P("space", "section"), P("space", "section")),
        check_vma=False,
    )
```

```python
import jax
import jax.numpy as jnp
from jax import lax
from jax.experimental import pallas as pl
from jax.experimental.pallas import tpu as pltpu
from jax.sharding import PartitionSpec as P

CA = 32
CB = 64
CC = 128
TAPS = 27
SLOPE = 0.3
BF16 = jnp.bfloat16
F32 = jnp.float32


def round_up(value, step):
    return -(-value // step) * step


def leaky(condition, value):
    return jnp.where(condition > 0, value, SLOPE * value)


def contract(a, b, dim_a, dim_b):
    return lax.dot_general(a, b, (((dim_a,), (dim_b,)), ((), ())), preferred_element_type=F32)


def call(body, out_shape, scratch, args):
    vmem = pl.BlockSpec(memory_space=pltpu.VMEM)
    many = isinstance(out_shape, (list, tuple))
    return pl.pallas_call(
        body,
        out_shape=out_shape,
        in_specs=[vmem] * len(args),
        out_specs=[vmem] * len(out_shape) if many else vmem,
        scratch_shapes=scratch,
        compiler_params=pltpu.CompilerParams(vmem_limit_bytes=32 << 20),
    )(*args)


def banded_body(weight, banded):
    lane = lax.broadcasted_iota(jnp.int32, (CA, 2 * CB), 1)
    zero = jnp.zeros((CA, 2 * CB), F32)
    turned = weight[...].astype(F32).T
    turned = jnp.concatenate([turned, turned], axis=1)
    for tap in range(9):
        left, right = [], []
        for kz in range(3):
            start = (3 * tap + kz) * CA
            both = turned[start : start + CA]
            left.append(jnp.where(lane < CB, both, 0.0))
            right.append(jnp.where(lane < CB, 0.0, both))
        for half in range(2):
            rows = []
            for z in range(8):
                block = zero
                for odd, side in ((0, left), (1, right)):
                    kz = z - 2 * (2 * half + odd) + 1
                    if 0 <= kz <= 2:
                        block = block + side[kz]
                rows.append(block)
            banded[pl.ds(tap * 256, 256), half * 128 : half * 128 + 128] = jnp.concatenate(
                rows, axis=0
            ).astype(BF16)


def main_body(count, spread, mine, got, before, upstream, banded, second, keep, send, xf, hid, hgs, t2, t1):
    side = lax.axis_index("space") % 2
    section = lax.axis_index("section")
    rows = count * 4
    planes = [before[i] for i in range(3)]
    own, other = [mine[0], mine[1]], [got[0], got[1]]
    first = side == 0
    planes += [jnp.where(first, own[i], other[i]) for i in range(2)]
    planes += [jnp.where(first, other[i], own[i]) for i in range(2)]
    row = lax.broadcasted_iota(jnp.int32, (rows, 256), 0)
    tiles = []
    for i, plane in enumerate(planes):
        flat = plane.reshape(count * 8, 256).astype(F32)
        for h in range(2):
            xf[i, h, 0:8, :] = jnp.zeros((8, 128), F32)
            xf[i, h, pl.ds(8, count * 8), :] = flat[:, h * 128 : h * 128 + 128]
        triple = []
        for ky in range(3):
            part = jnp.concatenate(
                [xf[i, h, pl.ds(7 + ky, rows, stride=2), :] for h in range(2)], axis=1
            )
            if ky == 0:
                part = jnp.where(row % 4 == 0, 0.0, part)
            triple.append(part.astype(BF16))
        tiles.append(triple)
    columns = [
        jnp.concatenate([tiles[2 * i + kx][ky] for i in range(3)], axis=0)
        for kx in range(3)
        for ky in range(3)
    ]
    preact = jnp.dot(jnp.concatenate(columns, axis=1), banded[...], preferred_element_type=F32)
    hidden = leaky(preact, preact).astype(BF16).astype(F32)
    half = count * 2
    lane = lax.broadcasted_iota(jnp.int32, (half, 128), 1)
    low = lane < CB
    row2 = lax.broadcasted_iota(jnp.int32, (half, 128), 0)
    cols = []
    for kx in range(3):
        for h in range(2):
            hid[kx, h, 0:8, :] = jnp.zeros((8, 128), F32)
            hid[kx, h, pl.ds(8, rows), :] = hidden[
                kx * rows : kx * rows + rows, h * 128 : h * 128 + 128
            ]
        for ky in range(3):
            a = hid[kx, 0, pl.ds(7 + ky, half, stride=2), :]
            b = hid[kx, 1, pl.ds(7 + ky, half, stride=2), :]
            if ky == 0:
                a = jnp.where(row2 % 2 == 0, 0.0, a)
                b = jnp.where(row2 % 2 == 0, 0.0, b)
            ra = pltpu.roll(a, 64, 1)
            rb = pltpu.roll(b, 64, 1)
            zero_k = jnp.concatenate([jnp.where(low, 0.0, ra), ra[:, :CB]], axis=1)
            one_k = jnp.concatenate([jnp.where(low, ra, rb), rb[:, :CB]], axis=1)
            cols.append(jnp.concatenate([zero_k, one_k], axis=0).astype(BF16))
    out = jnp.zeros((2 * half, CC), F32)
    for tap in range(9):
        out = out + jnp.dot(
            cols[tap], second[pl.ds(tap * 192, 192), :], preferred_element_type=F32
        )
    up = upstream[...].reshape(half, 256).astype(F32)
    up = jnp.concatenate([up[:, :128], up[:, 128:]], axis=0)
    delta = leaky(out, up)
    delta_b = delta.astype(BF16)
    turned = jnp.where(section == 0, delta, pltpu.roll(delta, 64, 1)).astype(BF16)
    for tap in range(9):
        t2[pl.ds(tap * 192, 192), :] = contract(cols[tap], turned, 0, 0)
    row3 = lax.broadcasted_iota(jnp.int32, (2 * half, 128), 0)
    for kx in range(3):
        parts = []
        for ky in range(3):
            base = (3 * kx + ky) * 192
            c0 = contract(delta_b, second[pl.ds(base, 128), :], 1, 1)
            c1 = contract(delta_b, second[pl.ds(base + 128, 64), :], 1, 1)
            parts.append((c0, jnp.concatenate([c1, c1], axis=1)))
        odd = []
        for late, early in zip(parts[2], parts[0]):
            shifted = pltpu.roll(early, 2 * half - 1, 0)
            odd.append(late + jnp.where(row3 % 2 == 0, shifted, 0.0))
        for parity, (c0, c1) in enumerate((parts[1], odd)):
            turn = pltpu.roll(c0, 64, 1)
            k0, k1 = turn[:half], turn[half:]
            a = jnp.where(low, k0, c1[:half] + k1)
            b = jnp.where(low, k1, c1[half:])
            hgs[kx, 0, pl.ds(parity, half, stride=2), :] = a
            hgs[kx, 1, pl.ds(parity, half, stride=2), :] = b
    hidden_grad = jnp.concatenate(
        [jnp.concatenate([hgs[kx, h] for kx in range(3)], axis=0) for h in range(2)], axis=1
    )
    hidden_grad = hidden_grad.astype(BF16).astype(F32)
    delta_a = leaky(hidden, hidden_grad).astype(BF16)
    wide = lax.broadcasted_iota(jnp.int32, (96, 128), 1) < CB
    for tap in range(9):
        grid = contract(columns[tap], delta_a, 0, 0)
        g0, g1 = grid[:, :128], grid[:, 128:]
        left = jnp.concatenate([g1[96:128], g0[0:64] + g1[128:192]], axis=0)
        right = g0[32:128] + g1[160:256]
        fold = jnp.where(wide, left, right)
        fold = fold + pltpu.roll(fold, 64, 1)
        t1[pl.ds(tap * 96, 96), :] = jnp.where(section == 0, fold, pltpu.roll(fold, 32, 1))
    r2, r1 = TAPS * CB // spread, TAPS * CA // spread
    h2, h1 = packed_rows(spread)
    t2[pl.ds(TAPS * CB, t2.shape[0] - TAPS * CB), :] = jnp.zeros((t2.shape[0] - TAPS * CB, 128), F32)
    t1[pl.ds(TAPS * CA, t1.shape[0] - TAPS * CA), :] = jnp.zeros((t1.shape[0] - TAPS * CA, 128), F32)
    low2 = lax.broadcasted_iota(jnp.int32, (h2, 128), 1) < CB
    quarter = lax.broadcasted_iota(jnp.int32, (h1, 128), 1) // 32

    def block(ref, d, start, size):
        even = ref[pl.ds(2 * d * size[0] + start, size[1]), :]
        odd = ref[pl.ds((2 * d + 1) * size[0] + start, size[1]), :]
        return jnp.where(first, even, odd)

    for d in range(spread // 2):
        a = block(t2, d, 0, (r2, h2))
        b = block(t2, d, h2, (r2, h2))
        keep[d, 0:h2, :] = jnp.where(low2, a, pltpu.roll(b, 64, 1)).astype(BF16)
        send[d, 0:h2, :] = jnp.where(low2, pltpu.roll(a, 64, 1), b).astype(BF16)
        kept, sent = None, None
        for g in range(4):
            straight = block(t1, d, g * h1, (r1, h1))
            turn = pltpu.roll(straight, 32, 1)
            k, o = (straight, turn) if g % 2 == 0 else (turn, straight)
            kept = k if g == 0 else jnp.where(quarter == g, k, kept)
            sent = o if g == 0 else jnp.where(quarter == g, o, sent)
        keep[d, h2 : h2 + h1, :] = kept.astype(BF16)
        send[d, h2 : h2 + h1, :] = sent.astype(BF16)


def packed_rows(spread):
    r2, r1 = TAPS * CB // spread, TAPS * CA // spread
    return round_up(-(-r2 // 2), 16), round_up(-(-r1 // 4), 16)


def unpack_body(spread, mine, got, first_out, second_out, first_buf, second_buf, sems):
    r2, r1 = TAPS * CB // spread, TAPS * CA // spread
    h2, h1 = packed_rows(spread)
    total = mine[...].astype(F32) + got[...].astype(F32)
    top = total[:h2].T
    second_buf[...] = jnp.concatenate([top[:CB], top[CB:]], axis=1)[:, :r2]
    second_copy = pltpu.make_async_copy(second_buf, second_out, sems.at[0])
    second_copy.start()
    rest = total[h2:].T
    rest = jnp.concatenate([rest[32 * g : 32 * g + 32] for g in range(4)], axis=1)
    first_buf[...] = rest[:, :r1]
    first_copy = pltpu.make_async_copy(first_buf, first_out, sems.at[1])
    first_copy.start()
    second_copy.wait()
    first_copy.wait()


def swap_bit(count, bit):
    return [(i, i ^ (1 << bit)) for i in range(count)]


def pick(array, index, axis):
    return lax.dynamic_index_in_dim(array, index, axis, keepdims=False)


def shards(input_field, first_weight, second_weight, upstream_grad):
    micro_count, _, planes, volumes, rows_y, packed = input_field.shape
    spread = lax.axis_size("space")
    pairs = spread // 2
    space = lax.axis_index("space")
    section = lax.axis_index("section")
    side, pair = space % 2, space // 2

    partner = lax.ppermute(upstream_grad, "space", swap_bit(spread, 0))
    both = jnp.where(
        side == 0, jnp.stack([upstream_grad, partner], 4), jnp.stack([partner, upstream_grad], 4)
    )
    up = pick(both[:, 0, :, 0], section, 0)[:, None]
    bits = pairs.bit_length() - 1
    for bit in reversed(range(bits)):
        up = up.reshape(2, up.shape[0] // 2, *up.shape[1:])
        here = (pair >> bit) & 1
        kept = pick(up, here, 0)
        came = lax.ppermute(pick(up, 1 - here, 0), "space", swap_bit(spread, bit + 1))
        up = jnp.where(here == 0, jnp.stack([kept, came], 2), jnp.stack([came, kept], 2))
        up = up.reshape(up.shape[0], -1, *up.shape[3:])
    up = up.reshape(volumes, *up.shape[-2:])

    mine = pick(input_field[:, 0], section, 0)
    got = lax.ppermute(mine, "space", swap_bit(spread, 0))
    onward = jnp.where(
        side == 0,
        jnp.stack([mine[1], got[0], got[1]]),
        jnp.stack([got[1], mine[0], mine[1]]),
    )
    before = lax.ppermute(onward, "space", [(i, i + 2) for i in range(spread - 2)])

    banded = call(banded_body, jax.ShapeDtypeStruct((9 * 256, 256), BF16), [], (first_weight.T,))
    h2, h1 = packed_rows(spread)
    block = jax.ShapeDtypeStruct((pairs, h2 + h1, 128), BF16)
    kept, outgoing = call(
        lambda *refs: main_body(volumes, spread, *refs),
        [block, block],
        [
            pltpu.VMEM((7, 2, volumes * 8 + 16, 128), F32),
            pltpu.VMEM((3, 2, volumes * 4 + 16, 128), F32),
            pltpu.VMEM((3, 2, volumes * 4, 128), F32),
            pltpu.VMEM((TAPS * CB + 2 * h2, 128), F32),
            pltpu.VMEM((TAPS * CA + 4 * h1, 128), F32),
        ],
        (mine, got, before, up, banded, second_weight),
    )

    def added(a, b):
        return (a.astype(F32) + b.astype(F32)).astype(BF16)

    total = added(kept, lax.ppermute(outgoing, "section", swap_bit(2, 0)))
    for bit in range(bits):
        paired = total.reshape(total.shape[0] // 2, 2, *total.shape[1:])
        here = (pair >> bit) & 1
        kept = pick(paired, here, 1)
        came = lax.ppermute(pick(paired, 1 - here, 1), "space", swap_bit(spread, bit + 1))
        total = added(kept, came)
    total = total[0]
    replicas = lax.axis_size("dp")
    bit = 0
    while 1 << (bit + 1) < replicas:
        total = added(total, lax.ppermute(total, "dp", swap_bit(replicas, bit)))
        bit += 1
    came = lax.ppermute(total, "dp", swap_bit(replicas, bit))
    first_out = (CB // 2, TAPS * CA // spread)
    second_out = (CC // 2, TAPS * CB // spread)
    vmem, hbm = pl.BlockSpec(memory_space=pltpu.VMEM), pl.BlockSpec(memory_space=pl.ANY)
    first_grad, second_grad = pl.pallas_call(
        lambda *refs: unpack_body(spread, *refs),
        out_shape=[jax.ShapeDtypeStruct(first_out, F32), jax.ShapeDtypeStruct(second_out, F32)],
        in_specs=[vmem, vmem],
        out_specs=[hbm, hbm],
        scratch_shapes=[
            pltpu.VMEM(first_out, F32),
            pltpu.VMEM(second_out, F32),
            pltpu.SemaphoreType.DMA((2,)),
        ],
        compiler_params=pltpu.CompilerParams(vmem_limit_bytes=16 << 20),
    )(total, came)
    return (first_grad.T, second_grad.T)


def solution(mesh):
    return jax.shard_map(
        shards,
        mesh=mesh,
        in_specs=(
            P(None, "dp", "space", None, None, None),
            P(),
            P(),
            P(None, "dp", None, "space", None, None),
        ),
        out_specs=(P("space", "section"), P("space", "section")),
        check_vma=False,
    )
```

```python
import jax
import jax.numpy as jnp
from jax import lax
from jax.experimental import pallas as pl
from jax.experimental.pallas import tpu as pltpu
from jax.sharding import PartitionSpec as P

CA = 32
CB = 64
CC = 128
TAPS = 27
SLOPE = 0.3
SPAN = 2
BF16 = jnp.bfloat16
F32 = jnp.float32


def round_up(value, step):
    return -(-value // step) * step


def leaky(condition, value):
    return jnp.where(condition > 0, value, SLOPE * value)


def contract(a, b, dim_a, dim_b):
    return lax.dot_general(a, b, (((dim_a,), (dim_b,)), ((), ())), preferred_element_type=F32)


def call(body, out_shape, scratch, args):
    vmem = pl.BlockSpec(memory_space=pltpu.VMEM)
    many = isinstance(out_shape, (list, tuple))
    return pl.pallas_call(
        body,
        out_shape=out_shape,
        in_specs=[vmem] * len(args),
        out_specs=[vmem] * len(out_shape) if many else vmem,
        scratch_shapes=scratch,
        compiler_params=pltpu.CompilerParams(vmem_limit_bytes=32 << 20),
    )(*args)


def banded_body(weight, banded):
    lane = lax.broadcasted_iota(jnp.int32, (CA, 2 * CB), 1)
    zero = jnp.zeros((CA, 2 * CB), F32)
    turned = weight[...].astype(F32).T
    turned = jnp.concatenate([turned, turned], axis=1)
    for tap in range(9):
        left, right = [], []
        for kz in range(3):
            start = (3 * tap + kz) * CA
            both = turned[start : start + CA]
            left.append(jnp.where(lane < CB, both, 0.0))
            right.append(jnp.where(lane < CB, 0.0, both))
        for half in range(2):
            rows = []
            for z in range(8):
                block = zero
                for odd, side in ((0, left), (1, right)):
                    kz = z - 2 * (2 * half + odd) + 1
                    if 0 <= kz <= 2:
                        block = block + side[kz]
                rows.append(block)
            banded[pl.ds(tap * 256, 256), half * 128 : half * 128 + 128] = jnp.concatenate(
                rows, axis=0
            ).astype(BF16)


def cut_body(span, pairs, field, upstream, *outs):
    pair = lax.axis_index("space") // 2
    section = lax.axis_index("section")
    width = 2 * span

    def fill(out, k, micro):
        first = ((pair ^ k) // span) * width
        for i in range(2):
            out[pl.ds(i * width, width)] = field[micro, 0, i, pl.ds(first, width)]
        if k < span:
            rows = [upstream[micro, 0, p, 0, pl.ds(j, 1), :] for j in range(2) for p in range(pairs)]
            rows = jnp.concatenate([r.astype(F32) for r in rows], axis=0).astype(BF16)
            out[pl.ds(2 * width, pairs // 4)] = rows.reshape(pairs // 4, 8, 256)

    fill(outs[0], 0, section)
    for k in range(1, pairs):
        for micro in range(2):
            fill(outs[k].at[micro], k, micro)


def main_body(span, pairs, spread, mine, partner, *refs):
    received = refs[: pairs - 1]
    swapped, banded, second, keep, send, xf, hid, hgs, us, t2, t1 = refs[pairs - 1 :]
    space = lax.axis_index("space")
    side, pair = space % 2, space // 2
    section = lax.axis_index("section")
    width = 2 * span
    tail = pairs // 4
    base = width * 8 + 8
    total = 2 * pairs * width * 8
    for i in range(2):
        for h in range(2):
            xf[i, h, 0:base, :] = jnp.zeros((base, 128), F32)

    def place(load, k, at_side):
        there = pair ^ k
        start = pl.multiple_of(base + (2 * there + at_side) * (width * 8), 8)
        for i in range(2):
            tiles = load(i * width, width).reshape(width * 8, 256).astype(F32)
            for h in range(2):
                xf[i, h, pl.ds(start, width * 8), :] = tiles[:, h * 128 : h * 128 + 128]
        if k < span:
            rows = load(2 * width, tail).reshape(2 * pairs, 256).astype(F32)
            volume = 2 * (there % span) + at_side
            for j in range(2):
                for h in range(2):
                    us[h, pl.ds(2 * volume + j, pairs, stride=2 * width), :] = rows[
                        j * pairs : j * pairs + pairs, h * 128 : h * 128 + 128
                    ]

    place(lambda at, size: mine[pl.ds(at, size)], 0, side)
    place(lambda at, size: partner[pl.ds(at, size)], 0, 1 - side)
    offset = 0
    for k in range(1, pairs):
        ref = received[k - 1]
        place(lambda at, size: ref[section, pl.ds(at, size)], k, side ^ section)
        start = offset
        place(lambda at, size: swapped[pl.ds(start + at, size)], k, 1 - (side ^ section))
        offset += ref.shape[1]

    rows = total // 2
    row = lax.broadcasted_iota(jnp.int32, (rows, 256), 0)
    columns = []
    for kx in range(3):
        for ky in range(3):
            start = base + ky - 1 - (width * 8 if kx == 0 else 0)
            part = jnp.concatenate(
                [xf[0 if kx == 1 else 1, h, pl.ds(start, rows, stride=2), :] for h in range(2)],
                axis=1,
            )
            if ky == 0:
                part = jnp.where(row % 4 == 0, 0.0, part)
            columns.append(part.astype(BF16))
    preact = jnp.dot(jnp.concatenate(columns, axis=1), banded[...], preferred_element_type=F32)
    hidden = leaky(preact, preact).astype(BF16).astype(F32)
    step = width * 4
    base2 = step + 8
    for i in range(2):
        picked = jnp.concatenate(
            [hidden[(2 * n + i) * step : (2 * n + i + 1) * step] for n in range(pairs)], axis=0
        )
        for h in range(2):
            hid[i, h, 0:base2, :] = jnp.zeros((base2, 128), F32)
            hid[i, h, pl.ds(base2, pairs * step), :] = picked[:, h * 128 : h * 128 + 128]
    half = pairs * width * 2
    low = lax.broadcasted_iota(jnp.int32, (half, 128), 1) < CB
    row2 = lax.broadcasted_iota(jnp.int32, (half, 128), 0)
    cols = []
    for kx in range(3):
        for ky in range(3):
            start = base2 + ky - 1 - (step if kx == 0 else 0)
            a, b = [hid[0 if kx == 1 else 1, h, pl.ds(start, half, stride=2), :] for h in range(2)]
            if ky == 0:
                a = jnp.where(row2 % 2 == 0, 0.0, a)
                b = jnp.where(row2 % 2 == 0, 0.0, b)
            ra = pltpu.roll(a, 64, 1)
            rb = pltpu.roll(b, 64, 1)
            zero_k = jnp.concatenate([jnp.where(low, 0.0, ra), ra[:, :CB]], axis=1)
            one_k = jnp.concatenate([jnp.where(low, ra, rb), rb[:, :CB]], axis=1)
            cols.append(jnp.concatenate([zero_k, one_k], axis=0).astype(BF16))
    out = jnp.zeros((2 * half, CC), F32)
    for tap in range(9):
        out = out + jnp.dot(
            cols[tap], second[pl.ds(tap * 192, 192), :], preferred_element_type=F32
        )
    up = jnp.concatenate([us[0], us[1]], axis=0)
    delta = leaky(out, up)
    delta_b = delta.astype(BF16)
    turned = jnp.where(section == 0, delta, pltpu.roll(delta, 64, 1)).astype(BF16)
    for tap in range(9):
        t2[pl.ds(tap * 192, 192), :] = contract(cols[tap], turned, 0, 0)
    row3 = lax.broadcasted_iota(jnp.int32, (2 * half, 128), 0)
    next_y = row3 % 2 == 0
    next_x = row3 % half < half - 2 * width
    grads = []
    for tap in range(9):
        c0 = contract(delta_b, second[pl.ds(tap * 192, 128), :], 1, 1)
        c1 = contract(delta_b, second[pl.ds(tap * 192 + 128, 64), :], 1, 1)
        grads.append([c0, jnp.concatenate([c1, c1], axis=1)])

    def joined(late, early, distance, valid):
        return [
            l + jnp.where(valid, pltpu.roll(e, 2 * half - distance, 0), 0.0)
            for l, e in zip(late, early)
        ]

    for i in range(2):
        if i == 0:
            over_y = grads[3:6]
        else:
            over_y = [joined(grads[6 + ky], grads[ky], 2 * width, next_x) for ky in range(3)]
        for parity, (c0, c1) in enumerate((over_y[1], joined(over_y[2], over_y[0], 1, next_y))):
            turn = pltpu.roll(c0, 64, 1)
            k0, k1 = turn[:half], turn[half:]
            hgs[i, 0, pl.ds(parity, half, stride=2), :] = jnp.where(low, k0, c1[:half] + k1)
            hgs[i, 1, pl.ds(parity, half, stride=2), :] = jnp.where(low, k1, c1[half:])
    hidden_grad = jnp.concatenate(
        [
            jnp.concatenate(
                [hgs[n % 2, h, pl.ds(n // 2 * step, step), :] for n in range(2 * pairs)], axis=0
            )
            for h in range(2)
        ],
        axis=1,
    )
    hidden_grad = hidden_grad.astype(BF16).astype(F32)
    delta_a = leaky(hidden, hidden_grad).astype(BF16)
    wide = lax.broadcasted_iota(jnp.int32, (96, 128), 1) < CB
    for tap in range(9):
        grid = contract(columns[tap], delta_a, 0, 0)
        g0, g1 = grid[:, :128], grid[:, 128:]
        left = jnp.concatenate([g1[96:128], g0[0:64] + g1[128:192]], axis=0)
        right = g0[32:128] + g1[160:256]
        fold = jnp.where(wide, left, right)
        fold = fold + pltpu.roll(fold, 64, 1)
        t1[pl.ds(tap * 96, 96), :] = jnp.where(section == 0, fold, pltpu.roll(fold, 32, 1))
    r2, r1 = TAPS * CB // spread, TAPS * CA // spread
    h2, h1 = packed_rows(spread)
    t2[pl.ds(TAPS * CB, t2.shape[0] - TAPS * CB), :] = jnp.zeros((t2.shape[0] - TAPS * CB, 128), F32)
    t1[pl.ds(TAPS * CA, t1.shape[0] - TAPS * CA), :] = jnp.zeros((t1.shape[0] - TAPS * CA, 128), F32)
    low2 = lax.broadcasted_iota(jnp.int32, (h2, 128), 1) < CB
    quarter = lax.broadcasted_iota(jnp.int32, (h1, 128), 1) // 32
    within = space % width

    def block(ref, n, stride, start, size):
        found = ref[pl.ds(n * width * stride + start, size), :]
        for other in range(1, width):
            more = ref[pl.ds((n * width + other) * stride + start, size), :]
            found = jnp.where(within == other, more, found)
        return found

    for n in range(pairs // span):
        a = block(t2, n, r2, 0, h2)
        b = block(t2, n, r2, h2, h2)
        keep[n, 0:h2, :] = jnp.where(low2, a, pltpu.roll(b, 64, 1)).astype(BF16)
        send[n, 0:h2, :] = jnp.where(low2, pltpu.roll(a, 64, 1), b).astype(BF16)
        kept, sent = None, None
        for g in range(4):
            straight = block(t1, n, r1, g * h1, h1)
            turn = pltpu.roll(straight, 32, 1)
            k, o = (straight, turn) if g % 2 == 0 else (turn, straight)
            kept = k if g == 0 else jnp.where(quarter == g, k, kept)
            sent = o if g == 0 else jnp.where(quarter == g, o, sent)
        keep[n, h2 : h2 + h1, :] = kept.astype(BF16)
        send[n, h2 : h2 + h1, :] = sent.astype(BF16)


def packed_rows(spread):
    r2, r1 = TAPS * CB // spread, TAPS * CA // spread
    return round_up(-(-r2 // 2), 16), round_up(-(-r1 // 4), 16)


def unpack_body(spread, mine, got, first_out, second_out, first_buf, second_buf, sems):
    r2, r1 = TAPS * CB // spread, TAPS * CA // spread
    h2, h1 = packed_rows(spread)
    total = mine[...].astype(F32) + got[...].astype(F32)
    top = total[:h2].T
    second_buf[...] = jnp.concatenate([top[:CB], top[CB:]], axis=1)[:, :r2]
    second_copy = pltpu.make_async_copy(second_buf, second_out, sems.at[0])
    second_copy.start()
    rest = total[h2:].T
    rest = jnp.concatenate([rest[32 * g : 32 * g + 32] for g in range(4)], axis=1)
    first_buf[...] = rest[:, :r1]
    first_copy = pltpu.make_async_copy(first_buf, first_out, sems.at[1])
    first_copy.start()
    second_copy.wait()
    first_copy.wait()


def swap_bit(count, bit):
    return [(i, i ^ (1 << bit)) for i in range(count)]


def pick(array, index, axis):
    return lax.dynamic_index_in_dim(array, index, axis, keepdims=False)


def shards(input_field, first_weight, second_weight, upstream_grad):
    spread = lax.axis_size("space")
    pairs = spread // 2
    span = SPAN
    width = 2 * span
    tail = pairs // 4
    pair = lax.axis_index("space") // 2
    section = lax.axis_index("section")

    piece = lambda k: 2 * width + (tail if k < span else 0)
    mine, *outgoing = call(
        lambda *refs: cut_body(span, pairs, *refs),
        [jax.ShapeDtypeStruct((piece(0), 8, 256), BF16)]
        + [jax.ShapeDtypeStruct((2, piece(k), 8, 256), BF16) for k in range(1, pairs)],
        [],
        (input_field, upstream_grad),
    )
    received = [None] * (pairs - 1)
    for k in sorted(range(1, pairs), key=lambda k: (k != 2, -k)):
        route = [(2 * d + c, 2 * (d ^ (2 * k) ^ c) + c) for d in range(spread) for c in range(2)]
        received[k - 1] = lax.ppermute(outgoing[k - 1], ("space", "section"), route)
    partner = lax.ppermute(mine, "space", swap_bit(spread, 0))
    swapped = lax.ppermute(
        jnp.concatenate([pick(block, 1 - section, 0) for block in received]),
        "section",
        swap_bit(2, 0),
    )

    banded = call(banded_body, jax.ShapeDtypeStruct((9 * 256, 256), BF16), [], (first_weight.T,))
    h2, h1 = packed_rows(spread)
    block = jax.ShapeDtypeStruct((pairs // span, h2 + h1, 128), BF16)
    kept, outgoing = call(
        lambda *refs: main_body(span, pairs, spread, *refs),
        [block, block],
        [
            pltpu.VMEM((2, 2, (2 * pairs + 1) * width * 8 + 16, 128), F32),
            pltpu.VMEM((2, 2, (pairs + 1) * width * 4 + 16, 128), F32),
            pltpu.VMEM((2, 2, pairs * width * 4, 128), F32),
            pltpu.VMEM((2, pairs * width * 2, 128), F32),
            pltpu.VMEM((TAPS * CB + 2 * h2, 128), F32),
            pltpu.VMEM((TAPS * CA + 4 * h1, 128), F32),
        ],
        (mine, partner, *received, swapped, banded, second_weight),
    )

    def added(a, b):
        return (a.astype(F32) + b.astype(F32)).astype(BF16)

    total = added(kept, lax.ppermute(outgoing, "section", swap_bit(2, 0)))
    bit = span.bit_length() - 1
    while total.shape[0] > 1:
        paired = total.reshape(total.shape[0] // 2, 2, *total.shape[1:])
        here = (pair >> bit) & 1
        kept = pick(paired, here, 1)
        came = lax.ppermute(pick(paired, 1 - here, 1), "space", swap_bit(spread, bit + 1))
        total = added(kept, came)
        bit += 1
    total = total[0]
    replicas = lax.axis_size("dp")
    bit = 0
    while 1 << (bit + 1) < replicas:
        total = added(total, lax.ppermute(total, "dp", swap_bit(replicas, bit)))
        bit += 1
    came = lax.ppermute(total, "dp", swap_bit(replicas, bit))
    first_out = (CB // 2, TAPS * CA // spread)
    second_out = (CC // 2, TAPS * CB // spread)
    vmem, hbm = pl.BlockSpec(memory_space=pltpu.VMEM), pl.BlockSpec(memory_space=pl.ANY)
    first_grad, second_grad = pl.pallas_call(
        lambda *refs: unpack_body(spread, *refs),
        out_shape=[jax.ShapeDtypeStruct(first_out, F32), jax.ShapeDtypeStruct(second_out, F32)],
        in_specs=[vmem, vmem],
        out_specs=[hbm, hbm],
        scratch_shapes=[
            pltpu.VMEM(first_out, F32),
            pltpu.VMEM(second_out, F32),
            pltpu.SemaphoreType.DMA((2,)),
        ],
        compiler_params=pltpu.CompilerParams(vmem_limit_bytes=16 << 20),
    )(total, came)
    return (first_grad.T, second_grad.T)


def solution(mesh):
    return jax.shard_map(
        shards,
        mesh=mesh,
        in_specs=(
            P(None, "dp", "space", None, None, None),
            P(),
            P(),
            P(None, "dp", None, "space", None, None),
        ),
        out_specs=(P("space", "section"), P("space", "section")),
        check_vma=False,
    )
```

```python
import jax
import jax.numpy as jnp
from jax import lax
from jax.experimental import pallas as pl
from jax.experimental.pallas import tpu as pltpu
from jax.sharding import PartitionSpec as P

CA = 32
CB = 64
CC = 128
TAPS = 27
SLOPE = 0.3
SPAN = 2
BF16 = jnp.bfloat16
F32 = jnp.float32


def round_up(value, step):
    return -(-value // step) * step


def leaky(condition, value):
    return jnp.where(condition > 0, value, SLOPE * value)


def contract(a, b, dim_a, dim_b):
    return lax.dot_general(a, b, (((dim_a,), (dim_b,)), ((), ())), preferred_element_type=F32)


def call(body, out_shape, scratch, args, in_hbm=0):
    vmem, hbm = pl.BlockSpec(memory_space=pltpu.VMEM), pl.BlockSpec(memory_space=pl.ANY)
    many = isinstance(out_shape, (list, tuple))
    return pl.pallas_call(
        body,
        out_shape=out_shape,
        in_specs=[vmem] * (len(args) - in_hbm) + [hbm] * in_hbm,
        out_specs=[vmem] * len(out_shape) if many else vmem,
        scratch_shapes=scratch,
        compiler_params=pltpu.CompilerParams(vmem_limit_bytes=32 << 20),
    )(*args)


def banded_body(weight, banded):
    lane = lax.broadcasted_iota(jnp.int32, (CA, 2 * CB), 1)
    zero = jnp.zeros((CA, 2 * CB), F32)
    turned = weight[...].astype(F32).T
    turned = jnp.concatenate([turned, turned], axis=1)
    for tap in range(9):
        left, right = [], []
        for kz in range(3):
            start = (3 * tap + kz) * CA
            both = turned[start : start + CA]
            left.append(jnp.where(lane < CB, both, 0.0))
            right.append(jnp.where(lane < CB, 0.0, both))
        for half in range(2):
            rows = []
            for z in range(8):
                block = zero
                for odd, side in ((0, left), (1, right)):
                    kz = z - 2 * (2 * half + odd) + 1
                    if 0 <= kz <= 2:
                        block = block + side[kz]
                rows.append(block)
            banded[pl.ds(tap * 256, 256), half * 128 : half * 128 + 128] = jnp.concatenate(
                rows, axis=0
            ).astype(BF16)


def cut_body(span, pairs, offsets, field, *refs):
    pair = lax.axis_index("space") // 2
    section = lax.axis_index("section")
    width = 2 * span

    def fill(out, k, micro):
        first = ((pair ^ k) // span) * width
        for i in range(2):
            out[pl.ds(i * width, width)] = field[micro, 0, i, pl.ds(first, width)]
        if k < span:
            upstream = refs[0]
            rows = [upstream[micro, 0, p, 0, pl.ds(j, 1), :] for j in range(2) for p in range(pairs)]
            rows = jnp.concatenate([r.astype(F32) for r in rows], axis=0).astype(BF16)
            out[pl.ds(2 * width, pairs // 4)] = rows.reshape(pairs // 4, 8, 256)

    for k, out in zip(offsets, refs[-len(offsets) :]):
        if k == 0:
            fill(out, k, section)
        else:
            for micro in range(2):
                fill(out.at[micro], k, micro)


def main_body(span, pairs, spread, mine, partner, *refs):
    received = refs[: pairs - 1]
    swapped, banded, second_hbm, keep, send = refs[pairs - 1 : pairs + 4]
    second, second_sem, xf, hid, hgs, us, t2, t1 = refs[pairs + 4 :]
    second_copy = pltpu.make_async_copy(second_hbm, second, second_sem)
    second_copy.start()
    space = lax.axis_index("space")
    side, pair = space % 2, space // 2
    section = lax.axis_index("section")
    width = 2 * span
    tail = pairs // 4
    base = width * 8 + 8
    total = 2 * pairs * width * 8
    for i in range(2):
        for h in range(2):
            xf[i, h, 0:base, :] = jnp.zeros((base, 128), F32)

    def place(load, k, at_side):
        there = pair ^ k
        start = pl.multiple_of(base + (2 * there + at_side) * (width * 8), 8)
        for i in range(2):
            tiles = load(i * width, width).reshape(width * 8, 256).astype(F32)
            for h in range(2):
                xf[i, h, pl.ds(start, width * 8), :] = tiles[:, h * 128 : h * 128 + 128]
        if k < span:
            rows = load(2 * width, tail).reshape(2 * pairs, 256).astype(F32)
            volume = 2 * (there % span) + at_side
            for j in range(2):
                for h in range(2):
                    us[h, pl.ds(2 * volume + j, pairs, stride=2 * width), :] = rows[
                        j * pairs : j * pairs + pairs, h * 128 : h * 128 + 128
                    ]

    place(lambda at, size: mine[pl.ds(at, size)], 0, side)
    place(lambda at, size: partner[pl.ds(at, size)], 0, 1 - side)
    offset = 0
    for k in range(1, pairs):
        ref = received[k - 1]
        place(lambda at, size: ref[section, pl.ds(at, size)], k, side ^ section)
        start = offset
        place(lambda at, size: swapped[pl.ds(start + at, size)], k, 1 - (side ^ section))
        offset += ref.shape[1]

    rows = total // 2
    row = lax.broadcasted_iota(jnp.int32, (rows, 256), 0)
    columns = []
    for kx in range(3):
        for ky in range(3):
            start = base + ky - 1 - (width * 8 if kx == 0 else 0)
            part = jnp.concatenate(
                [xf[0 if kx == 1 else 1, h, pl.ds(start, rows, stride=2), :] for h in range(2)],
                axis=1,
            )
            if ky == 0:
                part = jnp.where(row % 4 == 0, 0.0, part)
            columns.append(part.astype(BF16))
    preact = jnp.dot(jnp.concatenate(columns, axis=1), banded[...], preferred_element_type=F32)
    hidden = leaky(preact, preact).astype(BF16).astype(F32)
    step = width * 4
    base2 = step + 8
    for i in range(2):
        picked = jnp.concatenate(
            [hidden[(2 * n + i) * step : (2 * n + i + 1) * step] for n in range(pairs)], axis=0
        )
        for h in range(2):
            hid[i, h, 0:base2, :] = jnp.zeros((base2, 128), F32)
            hid[i, h, pl.ds(base2, pairs * step), :] = picked[:, h * 128 : h * 128 + 128]
    half = pairs * width * 2
    low = lax.broadcasted_iota(jnp.int32, (half, 128), 1) < CB
    row2 = lax.broadcasted_iota(jnp.int32, (half, 128), 0)
    cols = []
    for kx in range(3):
        for ky in range(3):
            start = base2 + ky - 1 - (step if kx == 0 else 0)
            a, b = [hid[0 if kx == 1 else 1, h, pl.ds(start, half, stride=2), :] for h in range(2)]
            if ky == 0:
                a = jnp.where(row2 % 2 == 0, 0.0, a)
                b = jnp.where(row2 % 2 == 0, 0.0, b)
            ra = pltpu.roll(a, 64, 1)
            rb = pltpu.roll(b, 64, 1)
            zero_k = jnp.concatenate([jnp.where(low, 0.0, ra), ra[:, :CB]], axis=1)
            one_k = jnp.concatenate([jnp.where(low, ra, rb), rb[:, :CB]], axis=1)
            cols.append(jnp.concatenate([zero_k, one_k], axis=0).astype(BF16))
    out = jnp.zeros((2 * half, CC), F32)
    second_copy.wait()
    for tap in range(9):
        out = out + jnp.dot(
            cols[tap], second[pl.ds(tap * 192, 192), :], preferred_element_type=F32
        )
    up = jnp.concatenate([us[0], us[1]], axis=0)
    delta = leaky(out, up)
    delta_b = delta.astype(BF16)
    turned = jnp.where(section == 0, delta, pltpu.roll(delta, 64, 1)).astype(BF16)
    for tap in range(9):
        t2[pl.ds(tap * 192, 192), :] = contract(cols[tap], turned, 0, 0)
    row3 = lax.broadcasted_iota(jnp.int32, (2 * half, 128), 0)
    next_y = row3 % 2 == 0
    next_x = row3 % half < half - 2 * width
    grads = []
    for tap in range(9):
        c0 = contract(delta_b, second[pl.ds(tap * 192, 128), :], 1, 1)
        c1 = contract(delta_b, second[pl.ds(tap * 192 + 128, 64), :], 1, 1)
        grads.append([c0, jnp.concatenate([c1, c1], axis=1)])

    def joined(late, early, distance, valid):
        return [
            l + jnp.where(valid, pltpu.roll(e, 2 * half - distance, 0), 0.0)
            for l, e in zip(late, early)
        ]

    for i in range(2):
        if i == 0:
            over_y = grads[3:6]
        else:
            over_y = [joined(grads[6 + ky], grads[ky], 2 * width, next_x) for ky in range(3)]
        for parity, (c0, c1) in enumerate((over_y[1], joined(over_y[2], over_y[0], 1, next_y))):
            turn = pltpu.roll(c0, 64, 1)
            k0, k1 = turn[:half], turn[half:]
            hgs[i, 0, pl.ds(parity, half, stride=2), :] = jnp.where(low, k0, c1[:half] + k1)
            hgs[i, 1, pl.ds(parity, half, stride=2), :] = jnp.where(low, k1, c1[half:])
    hidden_grad = jnp.concatenate(
        [
            jnp.concatenate(
                [hgs[n % 2, h, pl.ds(n // 2 * step, step), :] for n in range(2 * pairs)], axis=0
            )
            for h in range(2)
        ],
        axis=1,
    )
    hidden_grad = hidden_grad.astype(BF16).astype(F32)
    delta_a = leaky(hidden, hidden_grad).astype(BF16)
    wide = lax.broadcasted_iota(jnp.int32, (96, 128), 1) < CB
    for tap in range(9):
        grid = contract(columns[tap], delta_a, 0, 0)
        g0, g1 = grid[:, :128], grid[:, 128:]
        left = jnp.concatenate([g1[96:128], g0[0:64] + g1[128:192]], axis=0)
        right = g0[32:128] + g1[160:256]
        fold = jnp.where(wide, left, right)
        fold = fold + pltpu.roll(fold, 64, 1)
        t1[pl.ds(tap * 96, 96), :] = jnp.where(section == 0, fold, pltpu.roll(fold, 32, 1))
    r2, r1 = TAPS * CB // spread, TAPS * CA // spread
    h2, h1 = packed_rows(spread)
    t2[pl.ds(TAPS * CB, t2.shape[0] - TAPS * CB), :] = jnp.zeros((t2.shape[0] - TAPS * CB, 128), F32)
    t1[pl.ds(TAPS * CA, t1.shape[0] - TAPS * CA), :] = jnp.zeros((t1.shape[0] - TAPS * CA, 128), F32)
    low2 = lax.broadcasted_iota(jnp.int32, (h2, 128), 1) < CB
    quarter = lax.broadcasted_iota(jnp.int32, (h1, 128), 1) // 32
    within = space % width

    def block(ref, n, stride, start, size):
        found = ref[pl.ds(n * width * stride + start, size), :]
        for other in range(1, width):
            more = ref[pl.ds((n * width + other) * stride + start, size), :]
            found = jnp.where(within == other, more, found)
        return found

    for n in range(pairs // span):
        a = block(t2, n, r2, 0, h2)
        b = block(t2, n, r2, h2, h2)
        keep[n, 0:h2, :] = jnp.where(low2, a, pltpu.roll(b, 64, 1)).astype(BF16)
        send[n, 0:h2, :] = jnp.where(low2, pltpu.roll(a, 64, 1), b).astype(BF16)
        kept, sent = None, None
        for g in range(4):
            straight = block(t1, n, r1, g * h1, h1)
            turn = pltpu.roll(straight, 32, 1)
            k, o = (straight, turn) if g % 2 == 0 else (turn, straight)
            kept = k if g == 0 else jnp.where(quarter == g, k, kept)
            sent = o if g == 0 else jnp.where(quarter == g, o, sent)
        keep[n, h2 : h2 + h1, :] = kept.astype(BF16)
        send[n, h2 : h2 + h1, :] = sent.astype(BF16)


def packed_rows(spread):
    r2, r1 = TAPS * CB // spread, TAPS * CA // spread
    return round_up(-(-r2 // 2), 16), round_up(-(-r1 // 4), 16)


def unpack_body(spread, mine, got, first_out, second_out, first_buf, second_buf, sems):
    r2, r1 = TAPS * CB // spread, TAPS * CA // spread
    h2, h1 = packed_rows(spread)
    total = mine[...].astype(F32) + got[...].astype(F32)
    top = total[:h2].T
    second_buf[...] = jnp.concatenate([top[:CB], top[CB:]], axis=1)[:, :r2]
    second_copy = pltpu.make_async_copy(second_buf, second_out, sems.at[0])
    second_copy.start()
    rest = total[h2:].T
    rest = jnp.concatenate([rest[32 * g : 32 * g + 32] for g in range(4)], axis=1)
    first_buf[...] = rest[:, :r1]
    first_copy = pltpu.make_async_copy(first_buf, first_out, sems.at[1])
    first_copy.start()
    second_copy.wait()
    first_copy.wait()


def swap_bit(count, bit):
    return [(i, i ^ (1 << bit)) for i in range(count)]


def pick(array, index, axis):
    return lax.dynamic_index_in_dim(array, index, axis, keepdims=False)


def shards(input_field, first_weight, second_weight, upstream_grad):
    spread = lax.axis_size("space")
    pairs = spread // 2
    span = SPAN
    width = 2 * span
    tail = pairs // 4
    pair = lax.axis_index("space") // 2
    section = lax.axis_index("section")

    piece = lambda k: 2 * width + (tail if k < span else 0)
    pieces = {}
    for offsets, operands in (
        (range(span, pairs), (input_field,)),
        (range(span), (input_field, upstream_grad)),
    ):
        if len(offsets) > 0:
            shapes = [
                jax.ShapeDtypeStruct(((2,) if k > 0 else ()) + (piece(k), 8, 256), BF16)
                for k in offsets
            ]
            body = lambda *refs, offsets=offsets: cut_body(span, pairs, offsets, *refs)
            pieces.update(zip(offsets, call(body, shapes, [], operands)))
    mine = pieces[0]
    received = [None] * (pairs - 1)
    for k in range(pairs - 1, 0, -1):
        route = [(2 * d + c, 2 * (d ^ (2 * k) ^ c) + c) for d in range(spread) for c in range(2)]
        received[k - 1] = lax.ppermute(pieces[k], ("space", "section"), route)
    partner = lax.ppermute(mine, "space", swap_bit(spread, 0))
    banded = call(banded_body, jax.ShapeDtypeStruct((9 * 256, 256), BF16), [], (first_weight.T,))
    outgoing = jnp.concatenate([pick(block, 1 - section, 0) for block in received])
    outgoing, partner, banded = lax.optimization_barrier((outgoing, partner, banded))
    swapped = lax.ppermute(outgoing, "section", swap_bit(2, 0))
    h2, h1 = packed_rows(spread)
    block = jax.ShapeDtypeStruct((pairs // span, h2 + h1, 128), BF16)
    kept, outgoing = call(
        lambda *refs: main_body(span, pairs, spread, *refs),
        [block, block],
        [
            pltpu.VMEM(second_weight.shape, BF16),
            pltpu.SemaphoreType.DMA,
            pltpu.VMEM((2, 2, (2 * pairs + 1) * width * 8 + 16, 128), F32),
            pltpu.VMEM((2, 2, (pairs + 1) * width * 4 + 16, 128), F32),
            pltpu.VMEM((2, 2, pairs * width * 4, 128), F32),
            pltpu.VMEM((2, pairs * width * 2, 128), F32),
            pltpu.VMEM((TAPS * CB + 2 * h2, 128), F32),
            pltpu.VMEM((TAPS * CA + 4 * h1, 128), F32),
        ],
        (mine, partner, *received, swapped, banded, second_weight),
        in_hbm=1,
    )

    def added(a, b):
        return (a.astype(F32) + b.astype(F32)).astype(BF16)

    total = added(kept, lax.ppermute(outgoing, "section", swap_bit(2, 0)))
    bit = span.bit_length() - 1
    while total.shape[0] > 1:
        paired = total.reshape(total.shape[0] // 2, 2, *total.shape[1:])
        here = (pair >> bit) & 1
        kept = pick(paired, here, 1)
        came = lax.ppermute(pick(paired, 1 - here, 1), "space", swap_bit(spread, bit + 1))
        total = added(kept, came)
        bit += 1
    total = total[0]
    replicas = lax.axis_size("dp")
    bit = 0
    while 1 << (bit + 1) < replicas:
        total = added(total, lax.ppermute(total, "dp", swap_bit(replicas, bit)))
        bit += 1
    came = lax.ppermute(total, "dp", swap_bit(replicas, bit))
    first_out = (CB // 2, TAPS * CA // spread)
    second_out = (CC // 2, TAPS * CB // spread)
    vmem, hbm = pl.BlockSpec(memory_space=pltpu.VMEM), pl.BlockSpec(memory_space=pl.ANY)
    first_grad, second_grad = pl.pallas_call(
        lambda *refs: unpack_body(spread, *refs),
        out_shape=[jax.ShapeDtypeStruct(first_out, F32), jax.ShapeDtypeStruct(second_out, F32)],
        in_specs=[vmem, vmem],
        out_specs=[hbm, hbm],
        scratch_shapes=[
            pltpu.VMEM(first_out, F32),
            pltpu.VMEM(second_out, F32),
            pltpu.SemaphoreType.DMA((2,)),
        ],
        compiler_params=pltpu.CompilerParams(vmem_limit_bytes=16 << 20),
    )(total, came)
    return (first_grad.T, second_grad.T)


def solution(mesh):
    return jax.shard_map(
        shards,
        mesh=mesh,
        in_specs=(
            P(None, "dp", "space", None, None, None),
            P(),
            P(),
            P(None, "dp", None, "space", None, None),
        ),
        out_specs=(P("space", "section"), P("space", "section")),
        check_vma=False,
    )
```

```python
import jax
import jax.numpy as jnp
from jax import lax
from jax.experimental import pallas as pl
from jax.experimental.pallas import tpu as pltpu
from jax.sharding import PartitionSpec as P

CA = 32
CB = 64
CC = 128
TAPS = 27
SLOPE = 0.3
SPAN = 2
BF16 = jnp.bfloat16
F32 = jnp.float32


def round_up(value, step):
    return -(-value // step) * step


def leaky(condition, value):
    return jnp.where(condition > 0, value, SLOPE * value)


def contract(a, b, dim_a, dim_b):
    return lax.dot_general(a, b, (((dim_a,), (dim_b,)), ((), ())), preferred_element_type=F32)


def call(body, out_shape, scratch, args):
    vmem = pl.BlockSpec(memory_space=pltpu.VMEM)
    many = isinstance(out_shape, (list, tuple))
    return pl.pallas_call(
        body,
        out_shape=out_shape,
        in_specs=[vmem] * len(args),
        out_specs=[vmem] * len(out_shape) if many else vmem,
        scratch_shapes=scratch,
        compiler_params=pltpu.CompilerParams(vmem_limit_bytes=32 << 20),
    )(*args)


def banded_body(weight, banded):
    lane = lax.broadcasted_iota(jnp.int32, (CA, 2 * CB), 1)
    zero = jnp.zeros((CA, 2 * CB), F32)
    turned = weight[...].astype(F32).T
    turned = jnp.concatenate([turned, turned], axis=1)
    for tap in range(9):
        left, right = [], []
        for kz in range(3):
            start = (3 * tap + kz) * CA
            both = turned[start : start + CA]
            left.append(jnp.where(lane < CB, both, 0.0))
            right.append(jnp.where(lane < CB, 0.0, both))
        for half in range(2):
            rows = []
            for z in range(8):
                block = zero
                for odd, side in ((0, left), (1, right)):
                    kz = z - 2 * (2 * half + odd) + 1
                    if 0 <= kz <= 2:
                        block = block + side[kz]
                rows.append(block)
            banded[pl.ds(tap * 256, 256), half * 128 : half * 128 + 128] = jnp.concatenate(
                rows, axis=0
            ).astype(BF16)


def cut_body(span, pairs, field_hbm, upstream_hbm, *refs):
    *outs, field, upstream, sems = refs
    pair = lax.axis_index("space") // 2
    section = lax.axis_index("section")
    width = 2 * span
    copies = [
        pltpu.make_async_copy(field_hbm.at[0], field.at[0], sems.at[0]),
        pltpu.make_async_copy(field_hbm.at[1], field.at[1], sems.at[1]),
        pltpu.make_async_copy(upstream_hbm, upstream, sems.at[2]),
    ]
    for copy in copies:
        copy.start()
    for copy in copies:
        copy.wait()

    def fill(out, k, micro):
        first = ((pair ^ k) // span) * width
        for i in range(2):
            out[pl.ds(i * width, width)] = field[micro, 0, i, pl.ds(first, width)]
        if k < span:
            rows = [upstream[micro, 0, p, 0, pl.ds(j, 1), :] for j in range(2) for p in range(pairs)]
            rows = jnp.concatenate([r.astype(F32) for r in rows], axis=0).astype(BF16)
            out[pl.ds(2 * width, pairs // 4)] = rows.reshape(pairs // 4, 8, 256)

    fill(outs[0], 0, section)
    for k in range(1, pairs):
        for micro in range(2):
            fill(outs[k].at[micro], k, micro)


def main_body(span, pairs, spread, mine, partner, *refs):
    received = refs[: pairs - 1]
    swapped, banded, second, keep, send, xf, hid, hgs, us, t2, t1 = refs[pairs - 1 :]
    space = lax.axis_index("space")
    side, pair = space % 2, space // 2
    section = lax.axis_index("section")
    width = 2 * span
    tail = pairs // 4
    base = width * 8 + 8
    total = 2 * pairs * width * 8
    for i in range(2):
        for h in range(2):
            xf[i, h, 0:base, :] = jnp.zeros((base, 128), F32)

    def place(load, k, at_side):
        there = pair ^ k
        start = pl.multiple_of(base + (2 * there + at_side) * (width * 8), 8)
        for i in range(2):
            tiles = load(i * width, width).reshape(width * 8, 256).astype(F32)
            for h in range(2):
                xf[i, h, pl.ds(start, width * 8), :] = tiles[:, h * 128 : h * 128 + 128]
        if k < span:
            rows = load(2 * width, tail).reshape(2 * pairs, 256).astype(F32)
            volume = 2 * (there % span) + at_side
            for j in range(2):
                for h in range(2):
                    us[h, pl.ds(2 * volume + j, pairs, stride=2 * width), :] = rows[
                        j * pairs : j * pairs + pairs, h * 128 : h * 128 + 128
                    ]

    place(lambda at, size: mine[pl.ds(at, size)], 0, side)
    place(lambda at, size: partner[pl.ds(at, size)], 0, 1 - side)
    offset = 0
    for k in swap_order(span, pairs):
        ref = received[k - 1]
        place(lambda at, size: ref[section, pl.ds(at, size)], k, side ^ section)
        start = offset
        place(lambda at, size: swapped[pl.ds(start + at, size)], k, 1 - (side ^ section))
        offset += ref.shape[1]

    rows = total // 2
    row = lax.broadcasted_iota(jnp.int32, (rows, 256), 0)
    columns = []
    for kx in range(3):
        for ky in range(3):
            start = base + ky - 1 - (width * 8 if kx == 0 else 0)
            part = jnp.concatenate(
                [xf[0 if kx == 1 else 1, h, pl.ds(start, rows, stride=2), :] for h in range(2)],
                axis=1,
            )
            if ky == 0:
                part = jnp.where(row % 4 == 0, 0.0, part)
            columns.append(part.astype(BF16))
    preact = jnp.dot(jnp.concatenate(columns, axis=1), banded[...], preferred_element_type=F32)
    hidden = leaky(preact, preact).astype(BF16).astype(F32)
    step = width * 4
    base2 = step + 8
    for i in range(2):
        picked = jnp.concatenate(
            [hidden[(2 * n + i) * step : (2 * n + i + 1) * step] for n in range(pairs)], axis=0
        )
        for h in range(2):
            hid[i, h, 0:base2, :] = jnp.zeros((base2, 128), F32)
            hid[i, h, pl.ds(base2, pairs * step), :] = picked[:, h * 128 : h * 128 + 128]
    half = pairs * width * 2
    low = lax.broadcasted_iota(jnp.int32, (half, 128), 1) < CB
    row2 = lax.broadcasted_iota(jnp.int32, (half, 128), 0)
    cols = []
    for kx in range(3):
        for ky in range(3):
            start = base2 + ky - 1 - (step if kx == 0 else 0)
            a, b = [hid[0 if kx == 1 else 1, h, pl.ds(start, half, stride=2), :] for h in range(2)]
            if ky == 0:
                a = jnp.where(row2 % 2 == 0, 0.0, a)
                b = jnp.where(row2 % 2 == 0, 0.0, b)
            ra = pltpu.roll(a, 64, 1)
            rb = pltpu.roll(b, 64, 1)
            zero_k = jnp.concatenate([jnp.where(low, 0.0, ra), ra[:, :CB]], axis=1)
            one_k = jnp.concatenate([jnp.where(low, ra, rb), rb[:, :CB]], axis=1)
            cols.append(jnp.concatenate([zero_k, one_k], axis=0).astype(BF16))
    out = jnp.zeros((2 * half, CC), F32)
    for tap in range(9):
        out = out + jnp.dot(
            cols[tap], second[pl.ds(tap * 192, 192), :], preferred_element_type=F32
        )
    up = jnp.concatenate([us[0], us[1]], axis=0)
    delta = leaky(out, up)
    delta_b = delta.astype(BF16)
    turned = jnp.where(section == 0, delta, pltpu.roll(delta, 64, 1)).astype(BF16)
    for tap in range(9):
        t2[pl.ds(tap * 192, 192), :] = contract(cols[tap], turned, 0, 0)
    row3 = lax.broadcasted_iota(jnp.int32, (2 * half, 128), 0)
    next_y = row3 % 2 == 0
    next_x = row3 % half < half - 2 * width
    grads = []
    for tap in range(9):
        c0 = contract(delta_b, second[pl.ds(tap * 192, 128), :], 1, 1)
        c1 = contract(delta_b, second[pl.ds(tap * 192 + 128, 64), :], 1, 1)
        grads.append([c0, jnp.concatenate([c1, c1], axis=1)])

    def joined(late, early, distance, valid):
        return [
            l + jnp.where(valid, pltpu.roll(e, 2 * half - distance, 0), 0.0)
            for l, e in zip(late, early)
        ]

    for i in range(2):
        if i == 0:
            over_y = grads[3:6]
        else:
            over_y = [joined(grads[6 + ky], grads[ky], 2 * width, next_x) for ky in range(3)]
        for parity, (c0, c1) in enumerate((over_y[1], joined(over_y[2], over_y[0], 1, next_y))):
            turn = pltpu.roll(c0, 64, 1)
            k0, k1 = turn[:half], turn[half:]
            hgs[i, 0, pl.ds(parity, half, stride=2), :] = jnp.where(low, k0, c1[:half] + k1)
            hgs[i, 1, pl.ds(parity, half, stride=2), :] = jnp.where(low, k1, c1[half:])
    hidden_grad = jnp.concatenate(
        [
            jnp.concatenate(
                [hgs[n % 2, h, pl.ds(n // 2 * step, step), :] for n in range(2 * pairs)], axis=0
            )
            for h in range(2)
        ],
        axis=1,
    )
    hidden_grad = hidden_grad.astype(BF16).astype(F32)
    delta_a = leaky(hidden, hidden_grad).astype(BF16)
    wide = lax.broadcasted_iota(jnp.int32, (96, 128), 1) < CB
    for tap in range(9):
        grid = contract(columns[tap], delta_a, 0, 0)
        g0, g1 = grid[:, :128], grid[:, 128:]
        left = jnp.concatenate([g1[96:128], g0[0:64] + g1[128:192]], axis=0)
        right = g0[32:128] + g1[160:256]
        fold = jnp.where(wide, left, right)
        fold = fold + pltpu.roll(fold, 64, 1)
        t1[pl.ds(tap * 96, 96), :] = jnp.where(section == 0, fold, pltpu.roll(fold, 32, 1))
    r2, r1 = TAPS * CB // spread, TAPS * CA // spread
    h2, h1 = packed_rows(spread)
    t2[pl.ds(TAPS * CB, t2.shape[0] - TAPS * CB), :] = jnp.zeros((t2.shape[0] - TAPS * CB, 128), F32)
    t1[pl.ds(TAPS * CA, t1.shape[0] - TAPS * CA), :] = jnp.zeros((t1.shape[0] - TAPS * CA, 128), F32)
    low2 = lax.broadcasted_iota(jnp.int32, (h2, 128), 1) < CB
    quarter = lax.broadcasted_iota(jnp.int32, (h1, 128), 1) // 32
    within = space % width

    def block(ref, n, stride, start, size):
        found = ref[pl.ds(n * width * stride + start, size), :]
        for other in range(1, width):
            more = ref[pl.ds((n * width + other) * stride + start, size), :]
            found = jnp.where(within == other, more, found)
        return found

    for n in range(pairs // span):
        a = block(t2, n, r2, 0, h2)
        b = block(t2, n, r2, h2, h2)
        keep[n, 0:h2, :] = jnp.where(low2, a, pltpu.roll(b, 64, 1)).astype(BF16)
        send[n, 0:h2, :] = jnp.where(low2, pltpu.roll(a, 64, 1), b).astype(BF16)
        kept, sent = None, None
        for g in range(4):
            straight = block(t1, n, r1, g * h1, h1)
            turn = pltpu.roll(straight, 32, 1)
            k, o = (straight, turn) if g % 2 == 0 else (turn, straight)
            kept = k if g == 0 else jnp.where(quarter == g, k, kept)
            sent = o if g == 0 else jnp.where(quarter == g, o, sent)
        keep[n, h2 : h2 + h1, :] = kept.astype(BF16)
        send[n, h2 : h2 + h1, :] = sent.astype(BF16)


def swap_order(span, pairs):
    return [*range(pairs - 1, span, -1), *range(1, span + 1)]


def packed_rows(spread):
    r2, r1 = TAPS * CB // spread, TAPS * CA // spread
    return round_up(-(-r2 // 2), 16), round_up(-(-r1 // 4), 16)


def unpack_body(spread, mine, got, first_out, second_out, first_buf, second_buf, sems):
    r2, r1 = TAPS * CB // spread, TAPS * CA // spread
    h2, h1 = packed_rows(spread)
    total = mine[...].astype(F32) + got[...].astype(F32)
    top = total[:h2].T
    second_buf[...] = jnp.concatenate([top[:CB], top[CB:]], axis=1)[:, :r2]
    second_copy = pltpu.make_async_copy(second_buf, second_out, sems.at[0])
    second_copy.start()
    rest = total[h2:].T
    rest = jnp.concatenate([rest[32 * g : 32 * g + 32] for g in range(4)], axis=1)
    first_buf[...] = rest[:, :r1]
    first_copy = pltpu.make_async_copy(first_buf, first_out, sems.at[1])
    first_copy.start()
    second_copy.wait()
    first_copy.wait()


def swap_bit(count, bit):
    return [(i, i ^ (1 << bit)) for i in range(count)]


def pick(array, index, axis):
    return lax.dynamic_index_in_dim(array, index, axis, keepdims=False)


def shards(input_field, first_weight, second_weight, upstream_grad):
    spread = lax.axis_size("space")
    pairs = spread // 2
    span = SPAN
    width = 2 * span
    tail = pairs // 4
    pair = lax.axis_index("space") // 2
    section = lax.axis_index("section")

    piece = lambda k: 2 * width + (tail if k < span else 0)
    hbm = pl.BlockSpec(memory_space=pltpu.HBM)
    pieces = pl.pallas_call(
        lambda *refs: cut_body(span, pairs, *refs),
        out_shape=[
            jax.ShapeDtypeStruct(((2,) if k > 0 else ()) + (piece(k), 8, 256), BF16)
            for k in range(pairs)
        ],
        in_specs=[hbm, hbm],
        out_specs=[pl.BlockSpec(memory_space=pltpu.VMEM)] * pairs,
        scratch_shapes=[
            pltpu.VMEM(input_field.shape, BF16),
            pltpu.VMEM(upstream_grad.shape, BF16),
            pltpu.SemaphoreType.DMA((3,)),
        ],
        compiler_params=pltpu.CompilerParams(vmem_limit_bytes=16 << 20),
    )(
        pltpu.with_memory_space_constraint(input_field, pltpu.HBM),
        pltpu.with_memory_space_constraint(upstream_grad, pltpu.HBM),
    )
    mine = pieces[0]
    received = [None] * (pairs - 1)
    for k in sorted(range(1, pairs), key=lambda k: (k < span, k)):
        route = [(2 * d + c, 2 * (d ^ (2 * k) ^ c) + c) for d in range(spread) for c in range(2)]
        received[k - 1] = lax.ppermute(pieces[k], ("space", "section"), route)
    partner = lax.ppermute(mine, "space", swap_bit(spread, 0))
    banded = call(banded_body, jax.ShapeDtypeStruct((9 * 256, 256), BF16), [], (first_weight.T,))
    outgoing = jnp.concatenate([pick(received[k - 1], 1 - section, 0) for k in swap_order(span, pairs)])
    outgoing, partner, banded = lax.optimization_barrier((outgoing, partner, banded))
    swapped = lax.ppermute(outgoing, "section", swap_bit(2, 0))
    h2, h1 = packed_rows(spread)
    block = jax.ShapeDtypeStruct((pairs // span, h2 + h1, 128), BF16)
    kept, outgoing = call(
        lambda *refs: main_body(span, pairs, spread, *refs),
        [block, block],
        [
            pltpu.VMEM((2, 2, (2 * pairs + 1) * width * 8 + 16, 128), F32),
            pltpu.VMEM((2, 2, (pairs + 1) * width * 4 + 16, 128), F32),
            pltpu.VMEM((2, 2, pairs * width * 4, 128), F32),
            pltpu.VMEM((2, pairs * width * 2, 128), F32),
            pltpu.VMEM((TAPS * CB + 2 * h2, 128), F32),
            pltpu.VMEM((TAPS * CA + 4 * h1, 128), F32),
        ],
        (mine, partner, *received, swapped, banded, second_weight),
    )

    def added(a, b):
        return (a.astype(F32) + b.astype(F32)).astype(BF16)

    total = added(kept, lax.ppermute(outgoing, "section", swap_bit(2, 0)))
    bit = span.bit_length() - 1
    while total.shape[0] > 1:
        paired = total.reshape(total.shape[0] // 2, 2, *total.shape[1:])
        here = (pair >> bit) & 1
        kept = pick(paired, here, 1)
        came = lax.ppermute(pick(paired, 1 - here, 1), "space", swap_bit(spread, bit + 1))
        total = added(kept, came)
        bit += 1
    total = total[0]
    replicas = lax.axis_size("dp")
    bit = 0
    while 1 << (bit + 1) < replicas:
        total = added(total, lax.ppermute(total, "dp", swap_bit(replicas, bit)))
        bit += 1
    came = lax.ppermute(total, "dp", swap_bit(replicas, bit))
    first_out = (CB // 2, TAPS * CA // spread)
    second_out = (CC // 2, TAPS * CB // spread)
    vmem = pl.BlockSpec(memory_space=pltpu.VMEM)
    first_grad, second_grad = pl.pallas_call(
        lambda *refs: unpack_body(spread, *refs),
        out_shape=[jax.ShapeDtypeStruct(first_out, F32), jax.ShapeDtypeStruct(second_out, F32)],
        in_specs=[vmem, vmem],
        out_specs=[hbm, hbm],
        scratch_shapes=[
            pltpu.VMEM(first_out, F32),
            pltpu.VMEM(second_out, F32),
            pltpu.SemaphoreType.DMA((2,)),
        ],
        compiler_params=pltpu.CompilerParams(vmem_limit_bytes=16 << 20),
    )(total, came)
    return (first_grad.T, second_grad.T)


def solution(mesh):
    return jax.shard_map(
        shards,
        mesh=mesh,
        in_specs=(
            P(None, "dp", "space", None, None, None),
            P(),
            P(),
            P(None, "dp", None, "space", None, None),
        ),
        out_specs=(P("space", "section"), P("space", "section")),
        check_vma=False,
    )
```

```python
import jax
import jax.numpy as jnp
from jax import lax
from jax.experimental import pallas as pl
from jax.experimental.pallas import tpu as pltpu
from jax.sharding import PartitionSpec as P

CA = 32
CB = 64
CC = 128
TAPS = 27
SLOPE = 0.3
BF16 = jnp.bfloat16
F32 = jnp.float32


def round_up(value, step):
    return -(-value // step) * step


def leaky(condition, value):
    return jnp.where(condition > 0, value, SLOPE * value)


def contract(a, b, dim_a, dim_b):
    return lax.dot_general(a, b, (((dim_a,), (dim_b,)), ((), ())), preferred_element_type=F32)


def call(body, out_shape, scratch, args):
    vmem = pl.BlockSpec(memory_space=pltpu.VMEM)
    many = isinstance(out_shape, (list, tuple))
    return pl.pallas_call(
        body,
        out_shape=out_shape,
        in_specs=[vmem] * len(args),
        out_specs=[vmem] * len(out_shape) if many else vmem,
        scratch_shapes=scratch,
        compiler_params=pltpu.CompilerParams(vmem_limit_bytes=32 << 20),
    )(*args)


def banded_body(weight, banded):
    lane = lax.broadcasted_iota(jnp.int32, (CA, 2 * CB), 1)
    zero = jnp.zeros((CA, 2 * CB), F32)
    turned = weight[...].astype(F32).T
    turned = jnp.concatenate([turned, turned], axis=1)
    for tap in range(9):
        left, right = [], []
        for kz in range(3):
            start = (3 * tap + kz) * CA
            both = turned[start : start + CA]
            left.append(jnp.where(lane < CB, both, 0.0))
            right.append(jnp.where(lane < CB, 0.0, both))
        for half in range(2):
            rows = []
            for z in range(8):
                block = zero
                for odd, side in ((0, left), (1, right)):
                    kz = z - 2 * (2 * half + odd) + 1
                    if 0 <= kz <= 2:
                        block = block + side[kz]
                rows.append(block)
            banded[pl.ds(tap * 256, 256), half * 128 : half * 128 + 128] = jnp.concatenate(
                rows, axis=0
            ).astype(BF16)


def group_of(pair, pairs):
    return jnp.minimum(pair, pairs - 1 - pair)


def cut_body(pairs, field_hbm, upstream_hbm, *refs):
    *outs, field, upstream, sems = refs
    pair = lax.axis_index("space") // 2
    section = lax.axis_index("section")
    copies = [
        pltpu.make_async_copy(field_hbm.at[0], field.at[0], sems.at[0]),
        pltpu.make_async_copy(field_hbm.at[1], field.at[1], sems.at[1]),
        pltpu.make_async_copy(upstream_hbm, upstream, sems.at[2]),
    ]
    for copy in copies:
        copy.start()
    for copy in copies:
        copy.wait()

    def fill(out, k, micro):
        lower = group_of(pair ^ k, pairs)
        for i in range(2):
            for upper, member in enumerate((lower, pairs - 1 - lower)):
                out[pl.ds(4 * i + 2 * upper, 2)] = field[micro, 0, i, pl.ds(2 * member, 2)]
        if k in (0, pairs - 1):
            rows = [upstream[micro, 0, p, 0, pl.ds(j, 1), :] for j in range(2) for p in range(pairs)]
            rows = jnp.concatenate([r.astype(F32) for r in rows], axis=0).astype(BF16)
            out[pl.ds(8, pairs // 4)] = rows.reshape(pairs // 4, 8, 256)
        else:
            out[pl.ds(8, pairs // 4)] = jnp.zeros((pairs // 4, 8, 256), BF16)

    fill(outs[0], 0, section)
    for k in range(1, pairs):
        for micro in range(2):
            fill(outs[k].at[micro], k, micro)


def main_body(pairs, spread, mine, partner, *refs):
    received = refs[: pairs - 1]
    swapped, banded, second, keep, send, xf, hid, hgs, us, t2, t1 = refs[pairs - 1 :]
    space = lax.axis_index("space")
    side, pair = space % 2, space // 2
    section = lax.axis_index("section")
    width = 4
    tail = pairs // 4
    base = width * 8 + 8
    total = 2 * pairs * width * 8
    for i in range(2):
        for h in range(2):
            xf[i, h, 0:base, :] = jnp.zeros((base, 128), F32)

    def place(load, k, at_side):
        there = pair ^ k
        start = pl.multiple_of(base + (2 * there + at_side) * (width * 8), 8)
        for i in range(2):
            tiles = load(i * width, width).reshape(width * 8, 256).astype(F32)
            for h in range(2):
                xf[i, h, pl.ds(start, width * 8), :] = tiles[:, h * 128 : h * 128 + 128]
        if k in (0, pairs - 1):
            rows = load(2 * width, tail).reshape(2 * pairs, 256).astype(F32)
            volume = 2 * (there // (pairs // 2)) + at_side
            for j in range(2):
                for h in range(2):
                    us[h, pl.ds(2 * volume + j, pairs, stride=2 * width), :] = rows[
                        j * pairs : j * pairs + pairs, h * 128 : h * 128 + 128
                    ]

    place(lambda at, size: mine[pl.ds(at, size)], 0, side)
    place(lambda at, size: partner[pl.ds(at, size)], 0, 1 - side)
    offset = 0
    for k in swap_order(pairs):
        ref = received[k - 1]
        place(lambda at, size: ref[section, pl.ds(at, size)], k, side ^ section)
        start = offset
        place(lambda at, size: swapped[pl.ds(start + at, size)], k, 1 - (side ^ section))
        offset += ref.shape[1]

    rows = total // 2
    row = lax.broadcasted_iota(jnp.int32, (rows, 256), 0)
    columns = []
    for kx in range(3):
        for ky in range(3):
            start = base + ky - 1 - (width * 8 if kx == 0 else 0)
            part = jnp.concatenate(
                [xf[0 if kx == 1 else 1, h, pl.ds(start, rows, stride=2), :] for h in range(2)],
                axis=1,
            )
            if ky == 0:
                part = jnp.where(row % 4 == 0, 0.0, part)
            columns.append(part.astype(BF16))
    preact = jnp.dot(jnp.concatenate(columns, axis=1), banded[...], preferred_element_type=F32)
    hidden = leaky(preact, preact).astype(BF16).astype(F32)
    step = width * 4
    base2 = step + 8
    for i in range(2):
        picked = jnp.concatenate(
            [hidden[(2 * n + i) * step : (2 * n + i + 1) * step] for n in range(pairs)], axis=0
        )
        for h in range(2):
            hid[i, h, 0:base2, :] = jnp.zeros((base2, 128), F32)
            hid[i, h, pl.ds(base2, pairs * step), :] = picked[:, h * 128 : h * 128 + 128]
    half = pairs * width * 2
    low = lax.broadcasted_iota(jnp.int32, (half, 128), 1) < CB
    row2 = lax.broadcasted_iota(jnp.int32, (half, 128), 0)
    cols = []
    for kx in range(3):
        for ky in range(3):
            start = base2 + ky - 1 - (step if kx == 0 else 0)
            a, b = [hid[0 if kx == 1 else 1, h, pl.ds(start, half, stride=2), :] for h in range(2)]
            if ky == 0:
                a = jnp.where(row2 % 2 == 0, 0.0, a)
                b = jnp.where(row2 % 2 == 0, 0.0, b)
            ra = pltpu.roll(a, 64, 1)
            rb = pltpu.roll(b, 64, 1)
            zero_k = jnp.concatenate([jnp.where(low, 0.0, ra), ra[:, :CB]], axis=1)
            one_k = jnp.concatenate([jnp.where(low, ra, rb), rb[:, :CB]], axis=1)
            cols.append(jnp.concatenate([zero_k, one_k], axis=0).astype(BF16))
    out = jnp.zeros((2 * half, CC), F32)
    for tap in range(9):
        out = out + jnp.dot(
            cols[tap], second[pl.ds(tap * 192, 192), :], preferred_element_type=F32
        )
    up = jnp.concatenate([us[0], us[1]], axis=0)
    delta = leaky(out, up)
    delta_b = delta.astype(BF16)
    turned = jnp.where(section == 0, delta, pltpu.roll(delta, 64, 1)).astype(BF16)
    for tap in range(9):
        t2[pl.ds(tap * 192, 192), :] = contract(cols[tap], turned, 0, 0)
    row3 = lax.broadcasted_iota(jnp.int32, (2 * half, 128), 0)
    next_y = row3 % 2 == 0
    next_x = row3 % half < half - 2 * width
    grads = []
    for tap in range(9):
        c0 = contract(delta_b, second[pl.ds(tap * 192, 128), :], 1, 1)
        c1 = contract(delta_b, second[pl.ds(tap * 192 + 128, 64), :], 1, 1)
        grads.append([c0, jnp.concatenate([c1, c1], axis=1)])

    def joined(late, early, distance, valid):
        return [
            l + jnp.where(valid, pltpu.roll(e, 2 * half - distance, 0), 0.0)
            for l, e in zip(late, early)
        ]

    for i in range(2):
        if i == 0:
            over_y = grads[3:6]
        else:
            over_y = [joined(grads[6 + ky], grads[ky], 2 * width, next_x) for ky in range(3)]
        for parity, (c0, c1) in enumerate((over_y[1], joined(over_y[2], over_y[0], 1, next_y))):
            turn = pltpu.roll(c0, 64, 1)
            k0, k1 = turn[:half], turn[half:]
            hgs[i, 0, pl.ds(parity, half, stride=2), :] = jnp.where(low, k0, c1[:half] + k1)
            hgs[i, 1, pl.ds(parity, half, stride=2), :] = jnp.where(low, k1, c1[half:])
    hidden_grad = jnp.concatenate(
        [
            jnp.concatenate(
                [hgs[n % 2, h, pl.ds(n // 2 * step, step), :] for n in range(2 * pairs)], axis=0
            )
            for h in range(2)
        ],
        axis=1,
    )
    hidden_grad = hidden_grad.astype(BF16).astype(F32)
    delta_a = leaky(hidden, hidden_grad).astype(BF16)
    wide = lax.broadcasted_iota(jnp.int32, (96, 128), 1) < CB
    for tap in range(9):
        grid = contract(columns[tap], delta_a, 0, 0)
        g0, g1 = grid[:, :128], grid[:, 128:]
        left = jnp.concatenate([g1[96:128], g0[0:64] + g1[128:192]], axis=0)
        right = g0[32:128] + g1[160:256]
        fold = jnp.where(wide, left, right)
        fold = fold + pltpu.roll(fold, 64, 1)
        t1[pl.ds(tap * 96, 96), :] = jnp.where(section == 0, fold, pltpu.roll(fold, 32, 1))
    r2, r1 = TAPS * CB // spread, TAPS * CA // spread
    h2, h1 = packed_rows(spread)
    t2[pl.ds(TAPS * CB, t2.shape[0] - TAPS * CB), :] = jnp.zeros((t2.shape[0] - TAPS * CB, 128), F32)
    t1[pl.ds(TAPS * CA, t1.shape[0] - TAPS * CA), :] = jnp.zeros((t1.shape[0] - TAPS * CA, 128), F32)
    low2 = lax.broadcasted_iota(jnp.int32, (h2, 128), 1) < CB
    quarter = lax.broadcasted_iota(jnp.int32, (h1, 128), 1) // 32
    upper = pair // (pairs // 2)

    def block(ref, n, stride, start, size):
        found = None
        for member in range(2):
            for x in range(2):
                d = 2 * (pairs - 1 - n if member else n) + x
                more = ref[pl.ds(d * stride + start, size), :]
                here = jnp.logical_and(upper == member, side == x)
                found = more if found is None else jnp.where(here, more, found)
        return found

    for n in range(pairs // 2):
        a = block(t2, n, r2, 0, h2)
        b = block(t2, n, r2, h2, h2)
        keep[n, 0:h2, :] = jnp.where(low2, a, pltpu.roll(b, 64, 1)).astype(BF16)
        send[n, 0:h2, :] = jnp.where(low2, pltpu.roll(a, 64, 1), b).astype(BF16)
        kept, sent = None, None
        for g in range(4):
            straight = block(t1, n, r1, g * h1, h1)
            turn = pltpu.roll(straight, 32, 1)
            k, o = (straight, turn) if g % 2 == 0 else (turn, straight)
            kept = k if g == 0 else jnp.where(quarter == g, k, kept)
            sent = o if g == 0 else jnp.where(quarter == g, o, sent)
        keep[n, h2 : h2 + h1, :] = kept.astype(BF16)
        send[n, h2 : h2 + h1, :] = sent.astype(BF16)


def swap_order(pairs):
    return [1, 3, 2] if pairs == 4 else [*range(1, pairs)]


def packed_rows(spread):
    r2, r1 = TAPS * CB // spread, TAPS * CA // spread
    return round_up(-(-r2 // 2), 16), round_up(-(-r1 // 4), 16)


def unpack_body(spread, mine, got, first_out, second_out, first_buf, second_buf, sems):
    r2, r1 = TAPS * CB // spread, TAPS * CA // spread
    h2, h1 = packed_rows(spread)
    total = mine[...].astype(F32) + got[...].astype(F32)
    top = total[:h2].T
    second_buf[...] = jnp.concatenate([top[:CB], top[CB:]], axis=1)[:, :r2]
    second_copy = pltpu.make_async_copy(second_buf, second_out, sems.at[0])
    second_copy.start()
    rest = total[h2:].T
    rest = jnp.concatenate([rest[32 * g : 32 * g + 32] for g in range(4)], axis=1)
    first_buf[...] = rest[:, :r1]
    first_copy = pltpu.make_async_copy(first_buf, first_out, sems.at[1])
    first_copy.start()
    second_copy.wait()
    first_copy.wait()


def swap_bit(count, bit):
    return [(i, i ^ (1 << bit)) for i in range(count)]


def pick(array, index, axis):
    return lax.dynamic_index_in_dim(array, index, axis, keepdims=False)


def shards(input_field, first_weight, second_weight, upstream_grad):
    spread = lax.axis_size("space")
    pairs = spread // 2
    tail = pairs // 4
    pair = lax.axis_index("space") // 2
    section = lax.axis_index("section")

    piece = lambda k: 8 + tail
    hbm = pl.BlockSpec(memory_space=pltpu.HBM)
    pieces = pl.pallas_call(
        lambda *refs: cut_body(pairs, *refs),
        out_shape=[
            jax.ShapeDtypeStruct(((2,) if k > 0 else ()) + (piece(k), 8, 256), BF16)
            for k in range(pairs)
        ],
        in_specs=[hbm, hbm],
        out_specs=[pl.BlockSpec(memory_space=pltpu.VMEM)] * pairs,
        scratch_shapes=[
            pltpu.VMEM(input_field.shape, BF16),
            pltpu.VMEM(upstream_grad.shape, BF16),
            pltpu.SemaphoreType.DMA((3,)),
        ],
        compiler_params=pltpu.CompilerParams(vmem_limit_bytes=16 << 20),
    )(
        pltpu.with_memory_space_constraint(input_field, pltpu.HBM),
        pltpu.with_memory_space_constraint(upstream_grad, pltpu.HBM),
    )
    mine = pieces[0]
    received = [None] * (pairs - 1)
    for k in range(1, pairs):
        route = [(2 * d + c, 2 * (d ^ (2 * k) ^ c) + c) for d in range(spread) for c in range(2)]
        received[k - 1] = lax.ppermute(pieces[k], ("space", "section"), route)
    partner = lax.ppermute(mine, "space", swap_bit(spread, 0))
    banded = call(banded_body, jax.ShapeDtypeStruct((9 * 256, 256), BF16), [], (first_weight.T,))
    outgoing = jnp.concatenate([pick(received[k - 1], 1 - section, 0) for k in swap_order(pairs)])
    outgoing, partner, banded = lax.optimization_barrier((outgoing, partner, banded))
    swapped = lax.ppermute(outgoing, "section", swap_bit(2, 0))
    h2, h1 = packed_rows(spread)
    block = jax.ShapeDtypeStruct((pairs // 2, h2 + h1, 128), BF16)
    kept, outgoing = call(
        lambda *refs: main_body(pairs, spread, *refs),
        [block, block],
        [
            pltpu.VMEM((2, 2, (2 * pairs + 1) * 32 + 16, 128), F32),
            pltpu.VMEM((2, 2, (pairs + 1) * 16 + 16, 128), F32),
            pltpu.VMEM((2, 2, pairs * 16, 128), F32),
            pltpu.VMEM((2, pairs * 8, 128), F32),
            pltpu.VMEM((TAPS * CB + 2 * h2, 128), F32),
            pltpu.VMEM((TAPS * CA + 4 * h1, 128), F32),
        ],
        (mine, partner, *received, swapped, banded, second_weight),
    )

    def added(a, b):
        return (a.astype(F32) + b.astype(F32)).astype(BF16)

    total = added(kept, lax.ppermute(outgoing, "section", swap_bit(2, 0)))
    bit = 0
    while total.shape[0] > 1:
        paired = total.reshape(total.shape[0] // 2, 2, *total.shape[1:])
        here = (group_of(pair, pairs) >> bit) & 1
        kept = pick(paired, here, 1)
        came = lax.ppermute(pick(paired, 1 - here, 1), "space", swap_bit(spread, bit + 1))
        total = added(kept, came)
        bit += 1
    total = total[0]
    replicas = lax.axis_size("dp")
    bit = 0
    while 1 << (bit + 1) < replicas:
        total = added(total, lax.ppermute(total, "dp", swap_bit(replicas, bit)))
        bit += 1
    came = lax.ppermute(total, "dp", swap_bit(replicas, bit))
    first_out = (CB // 2, TAPS * CA // spread)
    second_out = (CC // 2, TAPS * CB // spread)
    vmem = pl.BlockSpec(memory_space=pltpu.VMEM)
    first_grad, second_grad = pl.pallas_call(
        lambda *refs: unpack_body(spread, *refs),
        out_shape=[jax.ShapeDtypeStruct(first_out, F32), jax.ShapeDtypeStruct(second_out, F32)],
        in_specs=[vmem, vmem],
        out_specs=[hbm, hbm],
        scratch_shapes=[
            pltpu.VMEM(first_out, F32),
            pltpu.VMEM(second_out, F32),
            pltpu.SemaphoreType.DMA((2,)),
        ],
        compiler_params=pltpu.CompilerParams(vmem_limit_bytes=16 << 20),
    )(total, came)
    return (first_grad.T, second_grad.T)


def solution(mesh):
    return jax.shard_map(
        shards,
        mesh=mesh,
        in_specs=(
            P(None, "dp", "space", None, None, None),
            P(),
            P(),
            P(None, "dp", None, "space", None, None),
        ),
        out_specs=(P("space", "section"), P("space", "section")),
        check_vma=False,
    )
```

```python
import jax
import jax.numpy as jnp
from jax import lax
from jax.experimental import pallas as pl
from jax.experimental.pallas import tpu as pltpu
from jax.sharding import PartitionSpec as P

CA = 32
CB = 64
CC = 128
TAPS = 27
SLOPE = 0.3
BF16 = jnp.bfloat16
F32 = jnp.float32


def round_up(value, step):
    return -(-value // step) * step


def leaky(condition, value):
    return jnp.where(condition > 0, value, SLOPE * value)


def contract(a, b, dim_a, dim_b):
    return lax.dot_general(a, b, (((dim_a,), (dim_b,)), ((), ())), preferred_element_type=F32)


def call(body, out_shape, scratch, args):
    vmem = pl.BlockSpec(memory_space=pltpu.VMEM)
    many = isinstance(out_shape, (list, tuple))
    return pl.pallas_call(
        body,
        out_shape=out_shape,
        in_specs=[vmem] * len(args),
        out_specs=[vmem] * len(out_shape) if many else vmem,
        scratch_shapes=scratch,
        compiler_params=pltpu.CompilerParams(vmem_limit_bytes=32 << 20),
    )(*args)


def banded_body(weight, banded):
    lane = lax.broadcasted_iota(jnp.int32, (CA, 2 * CB), 1)
    zero = jnp.zeros((CA, 2 * CB), F32)
    turned = weight[...].astype(F32).T
    turned = jnp.concatenate([turned, turned], axis=1)
    for tap in range(9):
        left, right = [], []
        for kz in range(3):
            start = (3 * tap + kz) * CA
            both = turned[start : start + CA]
            left.append(jnp.where(lane < CB, both, 0.0))
            right.append(jnp.where(lane < CB, 0.0, both))
        for half in range(2):
            rows = []
            for z in range(8):
                block = zero
                for odd, side in ((0, left), (1, right)):
                    kz = z - 2 * (2 * half + odd) + 1
                    if 0 <= kz <= 2:
                        block = block + side[kz]
                rows.append(block)
            banded[pl.ds(tap * 256, 256), half * 128 : half * 128 + 128] = jnp.concatenate(
                rows, axis=0
            ).astype(BF16)


def group_of(pair, pairs):
    return jnp.minimum(pair, pairs - 1 - pair)


def cut_body(pairs, field_hbm, upstream_hbm, *refs):
    *outs, field, upstream, sems = refs
    pair = lax.axis_index("space") // 2
    copies = [
        pltpu.make_async_copy(field_hbm.at[0], field.at[0], sems.at[0]),
        pltpu.make_async_copy(field_hbm.at[1], field.at[1], sems.at[1]),
        pltpu.make_async_copy(upstream_hbm, upstream, sems.at[2]),
    ]
    for copy in copies:
        copy.start()
    for copy in copies:
        copy.wait()

    def fill(out, k, micro):
        lower = group_of(pair ^ k, pairs)
        for i in range(2):
            for upper, member in enumerate((lower, pairs - 1 - lower)):
                out[pl.ds(4 * i + 2 * upper, 2)] = field[micro, 0, i, pl.ds(2 * member, 2)]
        if k in (0, pairs - 1):
            rows = [upstream[micro, 0, p, 0, pl.ds(j, 1), :] for j in range(2) for p in range(pairs)]
            rows = jnp.concatenate([r.astype(F32) for r in rows], axis=0).astype(BF16)
            out[pl.ds(8, pairs // 4)] = rows.reshape(pairs // 4, 8, 256)
        else:
            out[pl.ds(8, pairs // 4)] = jnp.zeros((pairs // 4, 8, 256), BF16)

    for k in range(pairs):
        for micro in range(2):
            fill(outs[k].at[micro], k, micro)
    outs[pairs][...] = outs[0][lax.axis_index("section")]


def main_body(pairs, spread, mine, partner, *refs):
    received = refs[: pairs - 1]
    swapped, banded, second, keep, xf, hid, hgs, us, t2, t1 = refs[pairs - 1 :]
    space = lax.axis_index("space")
    side, pair = space % 2, space // 2
    section = lax.axis_index("section")
    width = 8
    tail = pairs // 4
    base = width * 8 + 8
    total = 2 * pairs * width * 8
    for i in range(2):
        for h in range(2):
            xf[i, h, 0:base, :] = jnp.zeros((base, 128), F32)

    def place(load, k, at_side):
        there = pair ^ k
        start = pl.multiple_of(base + (2 * there + at_side) * (width * 8), 8)
        for micro in range(2):
            for i in range(2):
                tiles = load(micro, i * 4, 4).reshape(32, 256).astype(F32)
                for h in range(2):
                    xf[i, h, pl.ds(start + micro * 32, 32), :] = tiles[:, h * 128 : h * 128 + 128]
            if k in (0, pairs - 1):
                rows = load(micro, 8, tail).reshape(2 * pairs, 256).astype(F32)
                volume = 4 * micro + 2 * (there // (pairs // 2)) + at_side
                for j in range(2):
                    for h in range(2):
                        us[h, pl.ds(2 * volume + j, pairs, stride=2 * width), :] = rows[
                            j * pairs : j * pairs + pairs, h * 128 : h * 128 + 128
                        ]

    place(lambda micro, at, size: mine[micro, pl.ds(at, size)], 0, side)
    size_of = mine.shape[1]
    last = 2 * size_of * (pairs - 1)
    place(
        lambda micro, at, size: jnp.where(
            section == micro, partner[pl.ds(at, size)], swapped[pl.ds(last + at, size)]
        ),
        0,
        1 - side,
    )
    offset = 0
    for k in swap_order(pairs):
        ref = received[k - 1]
        place(lambda micro, at, size: ref[micro, pl.ds(at, size)], k, side ^ section)
        start = offset
        place(
            lambda micro, at, size: swapped[pl.ds(start + micro * size_of + at, size)],
            k,
            1 - (side ^ section),
        )
        offset += 2 * size_of

    rows = total // 2
    row = lax.broadcasted_iota(jnp.int32, (rows, 256), 0)
    columns = []
    for kx in range(3):
        for ky in range(3):
            start = base + ky - 1 - (width * 8 if kx == 0 else 0)
            part = jnp.concatenate(
                [xf[0 if kx == 1 else 1, h, pl.ds(start, rows, stride=2), :] for h in range(2)],
                axis=1,
            )
            if ky == 0:
                part = jnp.where(row % 4 == 0, 0.0, part)
            columns.append(part.astype(BF16))
    preact = jnp.dot(jnp.concatenate(columns, axis=1), banded[...], preferred_element_type=F32)
    hidden = leaky(preact, preact).astype(BF16).astype(F32)
    step = width * 4
    base2 = step + 8
    for i in range(2):
        picked = jnp.concatenate(
            [hidden[(2 * n + i) * step : (2 * n + i + 1) * step] for n in range(pairs)], axis=0
        )
        for h in range(2):
            hid[i, h, 0:base2, :] = jnp.zeros((base2, 128), F32)
            hid[i, h, pl.ds(base2, pairs * step), :] = picked[:, h * 128 : h * 128 + 128]
    half = pairs * width * 2
    low = lax.broadcasted_iota(jnp.int32, (half, 128), 1) < CB
    row2 = lax.broadcasted_iota(jnp.int32, (half, 128), 0)
    cols = []
    for kx in range(3):
        for ky in range(3):
            start = base2 + ky - 1 - (step if kx == 0 else 0)
            a, b = [hid[0 if kx == 1 else 1, h, pl.ds(start, half, stride=2), :] for h in range(2)]
            if ky == 0:
                a = jnp.where(row2 % 2 == 0, 0.0, a)
                b = jnp.where(row2 % 2 == 0, 0.0, b)
            ra = pltpu.roll(a, 64, 1)
            rb = pltpu.roll(b, 64, 1)
            zero_k = jnp.concatenate([jnp.where(low, 0.0, ra), ra[:, :CB]], axis=1)
            one_k = jnp.concatenate([jnp.where(low, ra, rb), rb[:, :CB]], axis=1)
            cols.append(jnp.concatenate([zero_k, one_k], axis=0).astype(BF16))
    out = jnp.zeros((2 * half, CC), F32)
    for tap in range(9):
        out = out + jnp.dot(
            cols[tap], second[pl.ds(tap * 192, 192), :], preferred_element_type=F32
        )
    up = jnp.concatenate([us[0], us[1]], axis=0)
    delta = leaky(out, up)
    delta_b = delta.astype(BF16)
    other = pltpu.roll(delta, 64, 1)
    low3 = lax.broadcasted_iota(jnp.int32, (2 * half, 128), 1) < CB
    turned = jnp.where(low3 == (section == 0), delta, other).astype(BF16)
    for tap in range(9):
        t2[pl.ds(tap * 192, 192), :] = contract(cols[tap], turned, 0, 0)
    row3 = lax.broadcasted_iota(jnp.int32, (2 * half, 128), 0)
    next_y = row3 % 2 == 0
    next_x = row3 % half < half - 2 * width
    grads = []
    for tap in range(9):
        c0 = contract(delta_b, second[pl.ds(tap * 192, 128), :], 1, 1)
        c1 = contract(delta_b, second[pl.ds(tap * 192 + 128, 64), :], 1, 1)
        grads.append([c0, jnp.concatenate([c1, c1], axis=1)])

    def joined(late, early, distance, valid):
        return [
            l + jnp.where(valid, pltpu.roll(e, 2 * half - distance, 0), 0.0)
            for l, e in zip(late, early)
        ]

    for i in range(2):
        if i == 0:
            over_y = grads[3:6]
        else:
            over_y = [joined(grads[6 + ky], grads[ky], 2 * width, next_x) for ky in range(3)]
        for parity, (c0, c1) in enumerate((over_y[1], joined(over_y[2], over_y[0], 1, next_y))):
            turn = pltpu.roll(c0, 64, 1)
            k0, k1 = turn[:half], turn[half:]
            hgs[i, 0, pl.ds(parity, half, stride=2), :] = jnp.where(low, k0, c1[:half] + k1)
            hgs[i, 1, pl.ds(parity, half, stride=2), :] = jnp.where(low, k1, c1[half:])
    hidden_grad = jnp.concatenate(
        [
            jnp.concatenate(
                [hgs[n % 2, h, pl.ds(n // 2 * step, step), :] for n in range(2 * pairs)], axis=0
            )
            for h in range(2)
        ],
        axis=1,
    )
    hidden_grad = hidden_grad.astype(BF16).astype(F32)
    delta_a = leaky(hidden, hidden_grad)
    quarters = lax.broadcasted_iota(jnp.int32, (rows, 128), 1) // 32
    even, late = delta_a[:, :128], delta_a[:, 128:]
    even = jnp.where(section == 0, even, pltpu.roll(even, 96, 1))
    late = jnp.where(section == 0, pltpu.roll(late, 32, 1), late)
    delta_a = jnp.where(quarters % 2 == 0, even, late).astype(BF16)
    quarter = lax.broadcasted_iota(jnp.int32, (96, 128), 1) // 32
    for tap in range(9):
        grid = contract(columns[tap], delta_a, 0, 0)
        fold = jnp.concatenate([jnp.zeros((32, 128), F32), grid[0:64]], axis=0)
        for q, k in ((1, 2), (2, 1), (3, 3)):
            fold = jnp.where(quarter == q, grid[64 * k - 32 : 64 * k + 64], fold)
        fold = fold + pltpu.roll(fold, 64, 1)
        t1[pl.ds(tap * 96, 96), :] = fold + pltpu.roll(fold, 32, 1)
    r2, r1 = TAPS * CB // spread, TAPS * CA // spread
    h2, h1 = packed_rows(spread)
    t2[pl.ds(TAPS * CB, t2.shape[0] - TAPS * CB), :] = jnp.zeros((t2.shape[0] - TAPS * CB, 128), F32)
    t1[pl.ds(TAPS * CA, t1.shape[0] - TAPS * CA), :] = jnp.zeros((t1.shape[0] - TAPS * CA, 128), F32)
    low2 = lax.broadcasted_iota(jnp.int32, (h2, 128), 1) < CB
    quarter = lax.broadcasted_iota(jnp.int32, (h1, 128), 1) // 32
    upper = pair // (pairs // 2)

    def block(ref, n, stride, start, size):
        found = None
        for member in range(2):
            for x in range(2):
                d = 2 * (pairs - 1 - n if member else n) + x
                more = ref[pl.ds(d * stride + start, size), :]
                here = jnp.logical_and(upper == member, side == x)
                found = more if found is None else jnp.where(here, more, found)
        return found

    for n in range(pairs // 2):
        a = block(t2, n, r2, 0, h2)
        b = block(t2, n, r2, h2, h2)
        keep[n, 0:h2, :] = jnp.where(low2, a, b).astype(BF16)
        kept = block(t1, n, r1, 0, h1)
        for g in range(1, 4):
            kept = jnp.where(quarter == g, block(t1, n, r1, g * h1, h1), kept)
        keep[n, h2 : h2 + h1, :] = kept.astype(BF16)


def swap_order(pairs):
    return [*range(2, 0, -1), *range(3, pairs)]


def packed_rows(spread):
    r2, r1 = TAPS * CB // spread, TAPS * CA // spread
    return round_up(-(-r2 // 2), 16), round_up(-(-r1 // 4), 16)


def unpack_body(spread, mine, got, first_out, second_out, first_buf, second_buf, sems):
    r2, r1 = TAPS * CB // spread, TAPS * CA // spread
    h2, h1 = packed_rows(spread)
    total = mine[...].astype(F32) + got[...].astype(F32)
    top = total[:h2].T
    second_buf[...] = jnp.concatenate([top[:CB], top[CB:]], axis=1)[:, :r2]
    second_copy = pltpu.make_async_copy(second_buf, second_out, sems.at[0])
    second_copy.start()
    rest = total[h2:].T
    rest = jnp.concatenate([rest[32 * g : 32 * g + 32] for g in range(4)], axis=1)
    first_buf[...] = rest[:, :r1]
    first_copy = pltpu.make_async_copy(first_buf, first_out, sems.at[1])
    first_copy.start()
    second_copy.wait()
    first_copy.wait()


def swap_bit(count, bit):
    return [(i, i ^ (1 << bit)) for i in range(count)]


def pick(array, index, axis):
    return lax.dynamic_index_in_dim(array, index, axis, keepdims=False)


def shards(input_field, first_weight, second_weight, upstream_grad):
    spread = lax.axis_size("space")
    pairs = spread // 2
    tail = pairs // 4
    pair = lax.axis_index("space") // 2

    hbm = pl.BlockSpec(memory_space=pltpu.HBM)
    pieces = pl.pallas_call(
        lambda *refs: cut_body(pairs, *refs),
        out_shape=[
            jax.ShapeDtypeStruct((2, 8 + tail, 8, 256), BF16)
            for k in range(pairs)
        ]
        + [jax.ShapeDtypeStruct((8 + tail, 8, 256), BF16)],
        in_specs=[hbm, hbm],
        out_specs=[pl.BlockSpec(memory_space=pltpu.VMEM)] * (pairs + 1),
        scratch_shapes=[
            pltpu.VMEM(input_field.shape, BF16),
            pltpu.VMEM(upstream_grad.shape, BF16),
            pltpu.SemaphoreType.DMA((3,)),
        ],
        compiler_params=pltpu.CompilerParams(vmem_limit_bytes=16 << 20),
    )(
        pltpu.with_memory_space_constraint(input_field, pltpu.HBM),
        pltpu.with_memory_space_constraint(upstream_grad, pltpu.HBM),
    )
    mine = pieces[0]
    received = [None] * (pairs - 1)
    for k in range(1, pairs):
        route = [(2 * d + c, 2 * (d ^ (2 * k) ^ c) + c) for d in range(spread) for c in range(2)]
        received[k - 1] = lax.ppermute(pieces[k], ("space", "section"), route)
    partner = lax.ppermute(pieces[pairs], "space", swap_bit(spread, 0))
    banded = call(banded_body, jax.ShapeDtypeStruct((9 * 256, 256), BF16), [], (first_weight.T,))
    outgoing = [received[k - 1].reshape(-1, 8, 256) for k in swap_order(pairs)] + [partner]
    outgoing, partner, banded = lax.optimization_barrier((jnp.concatenate(outgoing), partner, banded))
    swapped = lax.ppermute(outgoing, "section", swap_bit(2, 0))
    h2, h1 = packed_rows(spread)
    total = call(
        lambda *refs: main_body(pairs, spread, *refs),
        jax.ShapeDtypeStruct((pairs // 2, h2 + h1, 128), BF16),
        [
            pltpu.VMEM((2, 2, (2 * pairs + 1) * 64 + 16, 128), F32),
            pltpu.VMEM((2, 2, (pairs + 1) * 32 + 16, 128), F32),
            pltpu.VMEM((2, 2, pairs * 32, 128), F32),
            pltpu.VMEM((2, pairs * 16, 128), F32),
            pltpu.VMEM((TAPS * CB + 2 * h2, 128), F32),
            pltpu.VMEM((TAPS * CA + 4 * h1, 128), F32),
        ],
        (mine, partner, *received, swapped, banded, second_weight),
    )

    def added(a, b):
        return (a.astype(F32) + b.astype(F32)).astype(BF16)

    bit = 0
    while total.shape[0] > 1:
        paired = total.reshape(total.shape[0] // 2, 2, *total.shape[1:])
        here = (group_of(pair, pairs) >> bit) & 1
        kept = pick(paired, here, 1)
        came = lax.ppermute(pick(paired, 1 - here, 1), "space", swap_bit(spread, bit + 1))
        total = added(kept, came)
        bit += 1
    total = total[0]
    replicas = lax.axis_size("dp")
    bit = 0
    while 1 << (bit + 1) < replicas:
        total = added(total, lax.ppermute(total, "dp", swap_bit(replicas, bit)))
        bit += 1
    came = lax.ppermute(total, "dp", swap_bit(replicas, bit))
    first_out = (CB // 2, TAPS * CA // spread)
    second_out = (CC // 2, TAPS * CB // spread)
    vmem = pl.BlockSpec(memory_space=pltpu.VMEM)
    first_grad, second_grad = pl.pallas_call(
        lambda *refs: unpack_body(spread, *refs),
        out_shape=[jax.ShapeDtypeStruct(first_out, F32), jax.ShapeDtypeStruct(second_out, F32)],
        in_specs=[vmem, vmem],
        out_specs=[hbm, hbm],
        scratch_shapes=[
            pltpu.VMEM(first_out, F32),
            pltpu.VMEM(second_out, F32),
            pltpu.SemaphoreType.DMA((2,)),
        ],
        compiler_params=pltpu.CompilerParams(vmem_limit_bytes=16 << 20),
    )(total, came)
    return (first_grad.T, second_grad.T)


def solution(mesh):
    return jax.shard_map(
        shards,
        mesh=mesh,
        in_specs=(
            P(None, "dp", "space", None, None, None),
            P(),
            P(),
            P(None, "dp", None, "space", None, None),
        ),
        out_specs=(P("space", "section"), P("space", "section")),
        check_vma=False,
    )
```

```python
import jax
import jax.numpy as jnp
from jax import lax
from jax.experimental import pallas as pl
from jax.experimental.pallas import tpu as pltpu
from jax.sharding import PartitionSpec as P

CA = 32
CB = 64
CC = 128
TAPS = 27
SLOPE = 0.3
BF16 = jnp.bfloat16
F32 = jnp.float32


def round_up(value, step):
    return -(-value // step) * step


def leaky(condition, value):
    return jnp.where(condition > 0, value, SLOPE * value)


def contract(a, b, dim_a, dim_b):
    return lax.dot_general(a, b, (((dim_a,), (dim_b,)), ((), ())), preferred_element_type=F32)


def call(body, out_shape, scratch, args):
    vmem = pl.BlockSpec(memory_space=pltpu.VMEM)
    many = isinstance(out_shape, (list, tuple))
    return pl.pallas_call(
        body,
        out_shape=out_shape,
        in_specs=[vmem] * len(args),
        out_specs=[vmem] * len(out_shape) if many else vmem,
        scratch_shapes=scratch,
        compiler_params=pltpu.CompilerParams(vmem_limit_bytes=32 << 20),
    )(*args)


def weights_body(weight, second, banded, ordered):
    for tap in range(9):
        ordered[pl.ds(tap * 128, 128), :] = second[pl.ds(tap * 192, 128), :]
        ordered[pl.ds(1152 + tap * CB, CB), :] = second[pl.ds(tap * 192 + 128, CB), :]
    ordered[pl.ds(1152 + 9 * CB, CB), :] = jnp.zeros((CB, CC), BF16)
    lane = lax.broadcasted_iota(jnp.int32, (CA, 2 * CB), 1)
    zero = jnp.zeros((CA, 2 * CB), F32)
    turned = weight[...].astype(F32).T
    turned = jnp.concatenate([turned, turned], axis=1)
    for tap in range(9):
        left, right = [], []
        for kz in range(3):
            start = (3 * tap + kz) * CA
            both = turned[start : start + CA]
            left.append(jnp.where(lane < CB, both, 0.0))
            right.append(jnp.where(lane < CB, 0.0, both))
        for half in range(2):
            rows = []
            for z in range(8):
                block = zero
                for odd, side in ((0, left), (1, right)):
                    kz = z - 2 * (2 * half + odd) + 1
                    if 0 <= kz <= 2:
                        block = block + side[kz]
                rows.append(block)
            banded[pl.ds(tap * 256, 256), half * 128 : half * 128 + 128] = jnp.concatenate(
                rows, axis=0
            ).astype(BF16)


def group_of(pair, pairs):
    return jnp.minimum(pair, pairs - 1 - pair)


def cut_body(pairs, field_hbm, upstream_hbm, *refs):
    *outs, field, upstream, sems = refs
    pair = lax.axis_index("space") // 2
    copies = [
        pltpu.make_async_copy(field_hbm.at[m, 0, i], field.at[m, 0, i], sems.at[2 * m + i])
        for m in range(2)
        for i in range(2)
    ]
    copies.append(pltpu.make_async_copy(upstream_hbm, upstream, sems.at[4]))
    for copy in copies:
        copy.start()
    for copy in copies:
        copy.wait()

    def fill(out, k, micro):
        lower = group_of(pair ^ k, pairs)
        for i in range(2):
            for upper, member in enumerate((lower, pairs - 1 - lower)):
                out[pl.ds(4 * i + 2 * upper, 2)] = field[micro, 0, i, pl.ds(2 * member, 2)]
        if k in (0, pairs - 1):
            rows = [upstream[micro, 0, p, 0, pl.ds(j, 1), :] for j in range(2) for p in range(pairs)]
            rows = jnp.concatenate([r.astype(F32) for r in rows], axis=0).astype(BF16)
            out[pl.ds(8, pairs // 4)] = rows.reshape(pairs // 4, 8, 256)

    for k in range(pairs):
        for micro in range(2):
            fill(outs[k].at[micro], k, micro)
    outs[pairs][...] = outs[0][lax.axis_index("section")]


def main_body(pairs, spread, mine, partner, *refs):
    received = refs[: pairs - 1]
    swapped, banded, ordered, keep, xf, hid, hgs, us, t2, t1 = refs[pairs - 1 :]
    space = lax.axis_index("space")
    side, pair = space % 2, space // 2
    section = lax.axis_index("section")
    width = 8
    tail = pairs // 4
    base = width * 8 + 8
    total = 2 * pairs * width * 8
    for i in range(2):
        for h in range(2):
            xf[i, h, 0:base, :] = jnp.zeros((base, 128), F32)

    def place(load, k, at_side):
        there = pair ^ k
        start = pl.multiple_of(base + (2 * there + at_side) * (width * 8), 8)
        for micro in range(2):
            for i in range(2):
                tiles = load(micro, i * 4, 4).reshape(32, 256).astype(F32)
                for h in range(2):
                    xf[i, h, pl.ds(start + micro * 32, 32), :] = tiles[:, h * 128 : h * 128 + 128]
            if k in (0, pairs - 1):
                rows = load(micro, 8, tail).reshape(2 * pairs, 256).astype(F32)
                volume = 4 * micro + 2 * (there // (pairs // 2)) + at_side
                for j in range(2):
                    for h in range(2):
                        us[h, pl.ds(2 * volume + j, pairs, stride=2 * width), :] = rows[
                            j * pairs : j * pairs + pairs, h * 128 : h * 128 + 128
                        ]

    place(lambda micro, at, size: mine[micro, pl.ds(at, size)], 0, side)
    last = 2 * sum(ref.shape[1] for ref in received)
    place(
        lambda micro, at, size: jnp.where(
            section == micro, partner[pl.ds(at, size)], swapped[pl.ds(last + at, size)]
        ),
        0,
        1 - side,
    )
    offset = 0
    for k in swap_order(pairs):
        ref = received[k - 1]
        place(lambda micro, at, size: ref[micro, pl.ds(at, size)], k, side ^ section)
        start = offset
        place(
            lambda micro, at, size: swapped[pl.ds(start + micro * ref.shape[1] + at, size)],
            k,
            1 - (side ^ section),
        )
        offset += 2 * ref.shape[1]

    rows = total // 2
    row = lax.broadcasted_iota(jnp.int32, (rows, 256), 0)
    columns = []
    for kx in range(3):
        for ky in range(3):
            start = base + ky - 1 - (width * 8 if kx == 0 else 0)
            part = jnp.concatenate(
                [xf[0 if kx == 1 else 1, h, pl.ds(start, rows, stride=2), :] for h in range(2)],
                axis=1,
            )
            if ky == 0:
                part = jnp.where(row % 4 == 0, 0.0, part)
            columns.append(part.astype(BF16))
    preact = jnp.dot(jnp.concatenate(columns, axis=1), banded[...], preferred_element_type=F32)
    hidden = leaky(preact, preact).astype(BF16).astype(F32)
    step = width * 4
    base2 = step + 8
    for i in range(2):
        picked = jnp.concatenate(
            [hidden[(2 * n + i) * step : (2 * n + i + 1) * step] for n in range(pairs)], axis=0
        )
        for h in range(2):
            hid[i, h, 0:base2, :] = jnp.zeros((base2, 128), F32)
            hid[i, h, pl.ds(base2, pairs * step), :] = picked[:, h * 128 : h * 128 + 128]
    half = pairs * width * 2
    low = lax.broadcasted_iota(jnp.int32, (half, 128), 1) < CB
    row2 = lax.broadcasted_iota(jnp.int32, (half, 128), 0)
    cols, thirds = [], []
    for kx in range(3):
        for ky in range(3):
            start = base2 + ky - 1 - (step if kx == 0 else 0)
            a, b = [hid[0 if kx == 1 else 1, h, pl.ds(start, half, stride=2), :] for h in range(2)]
            if ky == 0:
                a = jnp.where(row2 % 2 == 0, 0.0, a)
                b = jnp.where(row2 % 2 == 0, 0.0, b)
            ra = pltpu.roll(a, 64, 1)
            rb = pltpu.roll(b, 64, 1)
            pair_k = [jnp.where(low, 0.0, ra), jnp.where(low, ra, rb)]
            cols.append(jnp.concatenate(pair_k, axis=0).astype(BF16))
            thirds.append((a, b) if len(thirds) % 2 else (ra, rb))
    thirds.append((0.0, 0.0))
    for p in range(5):
        pair_k = [jnp.where(low, f, l) for f, l in zip(thirds[2 * p], thirds[2 * p + 1])]
        cols.append(jnp.concatenate(pair_k, axis=0).astype(BF16))
    cols = jnp.concatenate(cols, axis=1)
    out = jnp.dot(cols, ordered[...], preferred_element_type=F32)
    up = jnp.concatenate([us[0], us[1]], axis=0)
    delta = leaky(out, up)
    delta_b = delta.astype(BF16)
    other = pltpu.roll(delta, 64, 1)
    low3 = lax.broadcasted_iota(jnp.int32, (2 * half, 128), 1) < CB
    turned = jnp.where(low3 == (section == 0), delta, other).astype(BF16)
    for two in range(7):
        grid = contract(cols[:, two * 256 : two * 256 + 256], turned, 0, 0)
        for tile in range(2):
            tap = 2 * two + tile
            if tap < 9:
                t2[pl.ds(tap * 192, 128), :] = grid[tile * 128 : tile * 128 + 128]
                continue
            for h in range(2):
                tap = 2 * (2 * two + tile - 9) + h
                if tap < 9:
                    row0 = tile * 128 + h * CB
                    t2[pl.ds(tap * 192 + 128, CB), :] = grid[row0 : row0 + CB]
    row3 = lax.broadcasted_iota(jnp.int32, (2 * half, 128), 0)
    next_y = row3 % 2 == 0
    next_x = row3 % half < half - 2 * width
    grid = contract(delta_b, ordered[...], 1, 1)
    grads = []
    for tap in range(9):
        c1 = grid[:, 1152 + tap // 2 * 128 : 1280 + tap // 2 * 128]
        c1 = c1 if tap % 2 else pltpu.roll(c1, 64, 1)
        grads.append([grid[:, tap * 128 : tap * 128 + 128], c1])

    def joined(late, early, distance, valid):
        return [
            l + jnp.where(valid, pltpu.roll(e, 2 * half - distance, 0), 0.0)
            for l, e in zip(late, early)
        ]

    for i in range(2):
        if i == 0:
            over_y = grads[3:6]
        else:
            over_y = [joined(grads[6 + ky], grads[ky], 2 * width, next_x) for ky in range(3)]
        for parity, (c0, c1) in enumerate((over_y[1], joined(over_y[2], over_y[0], 1, next_y))):
            turn = pltpu.roll(c0, 64, 1)
            k0, k1 = turn[:half], turn[half:]
            hgs[i, 0, pl.ds(parity, half, stride=2), :] = jnp.where(low, k0, c1[:half] + k1)
            hgs[i, 1, pl.ds(parity, half, stride=2), :] = jnp.where(low, k1, c1[half:])
    hidden_grad = jnp.concatenate(
        [
            jnp.concatenate(
                [hgs[n % 2, h, pl.ds(n // 2 * step, step), :] for n in range(2 * pairs)], axis=0
            )
            for h in range(2)
        ],
        axis=1,
    )
    hidden_grad = hidden_grad.astype(BF16).astype(F32)
    delta_a = leaky(hidden, hidden_grad)
    quarters = lax.broadcasted_iota(jnp.int32, (rows, 128), 1) // 32
    even, late = delta_a[:, :128], delta_a[:, 128:]
    even = jnp.where(section == 0, even, pltpu.roll(even, 96, 1))
    late = jnp.where(section == 0, pltpu.roll(late, 32, 1), late)
    delta_a = jnp.where(quarters % 2 == 0, even, late).astype(BF16)
    quarter = lax.broadcasted_iota(jnp.int32, (96, 128), 1) // 32
    for tap in range(9):
        grid = contract(columns[tap], delta_a, 0, 0)
        fold = jnp.concatenate([jnp.zeros((32, 128), F32), grid[0:64]], axis=0)
        for q, k in ((1, 2), (2, 1), (3, 3)):
            fold = jnp.where(quarter == q, grid[64 * k - 32 : 64 * k + 64], fold)
        fold = fold + pltpu.roll(fold, 64, 1)
        t1[pl.ds(tap * 96, 96), :] = fold + pltpu.roll(fold, 32, 1)
    r2, r1 = TAPS * CB // spread, TAPS * CA // spread
    h2, h1 = packed_rows(spread)
    t2[pl.ds(TAPS * CB, t2.shape[0] - TAPS * CB), :] = jnp.zeros((t2.shape[0] - TAPS * CB, 128), F32)
    t1[pl.ds(TAPS * CA, t1.shape[0] - TAPS * CA), :] = jnp.zeros((t1.shape[0] - TAPS * CA, 128), F32)
    low2 = lax.broadcasted_iota(jnp.int32, (h2, 128), 1) < CB
    quarter = lax.broadcasted_iota(jnp.int32, (h1, 128), 1) // 32
    upper = pair // (pairs // 2)

    def block(ref, n, stride, start, size):
        found = None
        for member in range(2):
            for x in range(2):
                d = 2 * (pairs - 1 - n if member else n) + x
                more = ref[pl.ds(d * stride + start, size), :]
                here = jnp.logical_and(upper == member, side == x)
                found = more if found is None else jnp.where(here, more, found)
        return found

    for n in range(pairs // 2):
        a = block(t2, n, r2, 0, h2)
        b = block(t2, n, r2, h2, h2)
        keep[n, 0:h2, :] = jnp.where(low2, a, b).astype(BF16)
        kept = block(t1, n, r1, 0, h1)
        for g in range(1, 4):
            kept = jnp.where(quarter == g, block(t1, n, r1, g * h1, h1), kept)
        keep[n, h2 : h2 + h1, :] = kept.astype(BF16)


def swap_order(pairs):
    return [*range(2, 0, -1), *range(3, pairs)]


def packed_rows(spread):
    r2, r1 = TAPS * CB // spread, TAPS * CA // spread
    return round_up(-(-r2 // 2), 16), round_up(-(-r1 // 4), 16)


def unpack_body(spread, mine, got, first_out, second_out, first_buf, second_buf, sems):
    r2, r1 = TAPS * CB // spread, TAPS * CA // spread
    h2, h1 = packed_rows(spread)
    total = mine[...].astype(F32) + got[...].astype(F32)
    top = total[:h2].T
    second_buf[...] = jnp.concatenate([top[:CB], top[CB:]], axis=1)[:, :r2]
    second_copy = pltpu.make_async_copy(second_buf, second_out, sems.at[0])
    second_copy.start()
    rest = total[h2:].T
    rest = jnp.concatenate([rest[32 * g : 32 * g + 32] for g in range(4)], axis=1)
    first_buf[...] = rest[:, :r1]
    first_copy = pltpu.make_async_copy(first_buf, first_out, sems.at[1])
    first_copy.start()
    second_copy.wait()
    first_copy.wait()


def swap_bit(count, bit):
    return [(i, i ^ (1 << bit)) for i in range(count)]


def pick(array, index, axis):
    return lax.dynamic_index_in_dim(array, index, axis, keepdims=False)


def shards(input_field, first_weight, second_weight, upstream_grad):
    spread = lax.axis_size("space")
    pairs = spread // 2
    tail = pairs // 4
    pair = lax.axis_index("space") // 2

    hbm = pl.BlockSpec(memory_space=pltpu.HBM)
    pieces = pl.pallas_call(
        lambda *refs: cut_body(pairs, *refs),
        out_shape=[
            jax.ShapeDtypeStruct((2, 8 + (tail if k in (0, pairs - 1) else 0), 8, 256), BF16)
            for k in range(pairs)
        ]
        + [jax.ShapeDtypeStruct((8 + tail, 8, 256), BF16)],
        in_specs=[hbm, hbm],
        out_specs=[pl.BlockSpec(memory_space=pltpu.VMEM)] * (pairs + 1),
        scratch_shapes=[
            pltpu.VMEM(input_field.shape, BF16),
            pltpu.VMEM(upstream_grad.shape, BF16),
            pltpu.SemaphoreType.DMA((5,)),
        ],
        compiler_params=pltpu.CompilerParams(vmem_limit_bytes=16 << 20),
    )(
        pltpu.with_memory_space_constraint(input_field, pltpu.HBM),
        pltpu.with_memory_space_constraint(upstream_grad, pltpu.HBM),
    )
    mine = pieces[0]
    received = [None] * (pairs - 1)
    for k in range(1, pairs):
        route = [(2 * d + c, 2 * (d ^ (2 * k) ^ c) + c) for d in range(spread) for c in range(2)]
        received[k - 1] = lax.ppermute(pieces[k], ("space", "section"), route)
    partner = lax.ppermute(pieces[pairs], "space", swap_bit(spread, 0))
    banded, ordered = call(
        weights_body,
        [
            jax.ShapeDtypeStruct((9 * 256, 256), BF16),
            jax.ShapeDtypeStruct((14 * 128, 128), BF16),
        ],
        [],
        (first_weight.T, second_weight),
    )
    outgoing = [received[k - 1].reshape(-1, 8, 256) for k in swap_order(pairs)] + [partner]
    outgoing, partner, banded = lax.optimization_barrier((jnp.concatenate(outgoing), partner, banded))
    swapped = lax.ppermute(outgoing, "section", swap_bit(2, 0))
    h2, h1 = packed_rows(spread)
    total = call(
        lambda *refs: main_body(pairs, spread, *refs),
        jax.ShapeDtypeStruct((pairs // 2, h2 + h1, 128), BF16),
        [
            pltpu.VMEM((2, 2, (2 * pairs + 1) * 64 + 16, 128), F32),
            pltpu.VMEM((2, 2, (pairs + 1) * 32 + 16, 128), F32),
            pltpu.VMEM((2, 2, pairs * 32, 128), F32),
            pltpu.VMEM((2, pairs * 16, 128), F32),
            pltpu.VMEM((TAPS * CB + 2 * h2, 128), F32),
            pltpu.VMEM((TAPS * CA + 4 * h1, 128), F32),
        ],
        (mine, partner, *received, swapped, banded, ordered),
    )

    def added(a, b):
        return (a.astype(F32) + b.astype(F32)).astype(BF16)

    bit = 0
    while total.shape[0] > 1:
        paired = total.reshape(total.shape[0] // 2, 2, *total.shape[1:])
        here = (group_of(pair, pairs) >> bit) & 1
        kept = pick(paired, here, 1)
        came = lax.ppermute(pick(paired, 1 - here, 1), "space", swap_bit(spread, bit + 1))
        total = added(kept, came)
        bit += 1
    total = total[0]
    replicas = lax.axis_size("dp")
    bit = 0
    while 1 << (bit + 1) < replicas:
        total = added(total, lax.ppermute(total, "dp", swap_bit(replicas, bit)))
        bit += 1
    came = lax.ppermute(total, "dp", swap_bit(replicas, bit))
    first_out = (CB // 2, TAPS * CA // spread)
    second_out = (CC // 2, TAPS * CB // spread)
    vmem = pl.BlockSpec(memory_space=pltpu.VMEM)
    first_grad, second_grad = pl.pallas_call(
        lambda *refs: unpack_body(spread, *refs),
        out_shape=[jax.ShapeDtypeStruct(first_out, F32), jax.ShapeDtypeStruct(second_out, F32)],
        in_specs=[vmem, vmem],
        out_specs=[hbm, hbm],
        scratch_shapes=[
            pltpu.VMEM(first_out, F32),
            pltpu.VMEM(second_out, F32),
            pltpu.SemaphoreType.DMA((2,)),
        ],
        compiler_params=pltpu.CompilerParams(vmem_limit_bytes=16 << 20),
    )(total, came)
    return (first_grad.T, second_grad.T)


def solution(mesh):
    return jax.shard_map(
        shards,
        mesh=mesh,
        in_specs=(
            P(None, "dp", "space", None, None, None),
            P(),
            P(),
            P(None, "dp", None, "space", None, None),
        ),
        out_specs=(P("space", "section"), P("space", "section")),
        check_vma=False,
    )
```

```python
import jax
import jax.numpy as jnp
from jax import lax
from jax.experimental import pallas as pl
from jax.experimental.pallas import tpu as pltpu
from jax.sharding import PartitionSpec as P

CA = 32
CB = 64
CC = 128
TAPS = 27
SLOPE = 0.3
BF16 = jnp.bfloat16
F32 = jnp.float32


def round_up(value, step):
    return -(-value // step) * step


def leaky(condition, value):
    return jnp.where(condition > 0, value, SLOPE * value)


def contract(a, b, dim_a, dim_b):
    return lax.dot_general(a, b, (((dim_a,), (dim_b,)), ((), ())), preferred_element_type=F32)


def call(body, out_shape, scratch, args):
    vmem = pl.BlockSpec(memory_space=pltpu.VMEM)
    many = isinstance(out_shape, (list, tuple))
    return pl.pallas_call(
        body,
        out_shape=out_shape,
        in_specs=[vmem] * len(args),
        out_specs=[vmem] * len(out_shape) if many else vmem,
        scratch_shapes=scratch,
        compiler_params=pltpu.CompilerParams(vmem_limit_bytes=32 << 20),
    )(*args)


def weights_body(weight_hbm, second_hbm, banded, ordered, weight, second, sems):
    copies = [
        pltpu.make_async_copy(weight_hbm, weight, sems.at[0]),
        pltpu.make_async_copy(second_hbm, second, sems.at[1]),
    ]
    for copy in copies:
        copy.start()
    for copy in copies:
        copy.wait()
    for tap in range(9):
        ordered[pl.ds(tap * 128, 128), :] = second[pl.ds(tap * 192, 128), :]
        ordered[pl.ds(1152 + tap * CB, CB), :] = second[pl.ds(tap * 192 + 128, CB), :]
    ordered[pl.ds(1152 + 9 * CB, CB), :] = jnp.zeros((CB, CC), BF16)
    lane = lax.broadcasted_iota(jnp.int32, (CA, 2 * CB), 1)
    zero = jnp.zeros((CA, 2 * CB), F32)
    turned = weight[...].astype(F32).T
    turned = jnp.concatenate([turned, turned], axis=1)
    for tap in range(9):
        left, right = [], []
        for kz in range(3):
            start = (3 * tap + kz) * CA
            both = turned[start : start + CA]
            left.append(jnp.where(lane < CB, both, 0.0))
            right.append(jnp.where(lane < CB, 0.0, both))
        for half in range(2):
            rows = []
            for z in range(8):
                block = zero
                for odd, side in ((0, left), (1, right)):
                    kz = z - 2 * (2 * half + odd) + 1
                    if 0 <= kz <= 2:
                        block = block + side[kz]
                rows.append(block)
            banded[pl.ds(tap * 256, 256), half * 128 : half * 128 + 128] = jnp.concatenate(
                rows, axis=0
            ).astype(BF16)


def group_of(pair, pairs):
    return jnp.minimum(pair, pairs - 1 - pair)


def cut_body(pairs, field_hbm, upstream_hbm, *refs):
    *outs, field, upstream, sems = refs
    pair = lax.axis_index("space") // 2
    copies = [
        pltpu.make_async_copy(field_hbm.at[m, 0, i], field.at[m, 0, i], sems.at[2 * m + i])
        for m in range(2)
        for i in range(2)
    ]
    copies.append(pltpu.make_async_copy(upstream_hbm, upstream, sems.at[4]))
    for copy in copies:
        copy.start()
    for copy in copies:
        copy.wait()

    def fill(out, k, micro):
        lower = group_of(pair ^ k, pairs)
        for i in range(2):
            for upper, member in enumerate((lower, pairs - 1 - lower)):
                out[pl.ds(4 * i + 2 * upper, 2)] = field[micro, 0, i, pl.ds(2 * member, 2)]
        if k in (0, pairs - 1):
            rows = [upstream[micro, 0, p, 0, pl.ds(j, 1), :] for j in range(2) for p in range(pairs)]
            rows = jnp.concatenate([r.astype(F32) for r in rows], axis=0).astype(BF16)
            out[pl.ds(8, pairs // 4)] = rows.reshape(pairs // 4, 8, 256)

    for k in range(pairs):
        for micro in range(2):
            fill(outs[k].at[micro], k, micro)
    outs[pairs][...] = outs[0][lax.axis_index("section")]


def main_body(pairs, spread, mine, partner, *refs):
    received = refs[: pairs - 1]
    early, late, banded, ordered, keep, xf, hid, hgs, us, t2, t1 = refs[pairs - 1 :]
    space = lax.axis_index("space")
    side, pair = space % 2, space // 2
    section = lax.axis_index("section")
    width = 8
    tail = pairs // 4
    base = width * 8 + 8
    total = 2 * pairs * width * 8
    for i in range(2):
        for h in range(2):
            xf[i, h, 0:base, :] = jnp.zeros((base, 128), F32)

    def place(load, k, at_side):
        there = pair ^ k
        start = pl.multiple_of(base + (2 * there + at_side) * (width * 8), 8)
        for micro in range(2):
            for i in range(2):
                tiles = load(micro, i * 4, 4).reshape(32, 256).astype(F32)
                for h in range(2):
                    xf[i, h, pl.ds(start + micro * 32, 32), :] = tiles[:, h * 128 : h * 128 + 128]
            if k in (0, pairs - 1):
                rows = load(micro, 8, tail).reshape(2 * pairs, 256).astype(F32)
                volume = 4 * micro + 2 * (there // (pairs // 2)) + at_side
                for j in range(2):
                    for h in range(2):
                        us[h, pl.ds(2 * volume + j, pairs, stride=2 * width), :] = rows[
                            j * pairs : j * pairs + pairs, h * 128 : h * 128 + 128
                        ]

    place(lambda micro, at, size: mine[micro, pl.ds(at, size)], 0, side)
    last = 2 * received[0].shape[1]
    place(
        lambda micro, at, size: jnp.where(
            section == micro, partner[pl.ds(at, size)], late[pl.ds(last + at, size)]
        ),
        0,
        1 - side,
    )
    offset = 0
    for k in [1] + swap_order(pairs):
        ref = received[k - 1]
        place(lambda micro, at, size: ref[micro, pl.ds(at, size)], k, side ^ section)
        swapped = late if k == 1 else early
        start = 0 if k == 1 else offset
        place(
            lambda micro, at, size: swapped[pl.ds(start + micro * ref.shape[1] + at, size)],
            k,
            1 - (side ^ section),
        )
        offset += 0 if k == 1 else 2 * ref.shape[1]

    rows = total // 2
    row = lax.broadcasted_iota(jnp.int32, (rows, 256), 0)
    columns = []
    for kx in range(3):
        for ky in range(3):
            start = base + ky - 1 - (width * 8 if kx == 0 else 0)
            part = jnp.concatenate(
                [xf[0 if kx == 1 else 1, h, pl.ds(start, rows, stride=2), :] for h in range(2)],
                axis=1,
            )
            if ky == 0:
                part = jnp.where(row % 4 == 0, 0.0, part)
            columns.append(part.astype(BF16))
    preact = jnp.dot(jnp.concatenate(columns, axis=1), banded[...], preferred_element_type=F32)
    hidden = leaky(preact, preact).astype(BF16).astype(F32)
    step = width * 4
    base2 = step + 8
    for i in range(2):
        picked = jnp.concatenate(
            [hidden[(2 * n + i) * step : (2 * n + i + 1) * step] for n in range(pairs)], axis=0
        )
        for h in range(2):
            hid[i, h, 0:base2, :] = jnp.zeros((base2, 128), F32)
            hid[i, h, pl.ds(base2, pairs * step), :] = picked[:, h * 128 : h * 128 + 128]
    half = pairs * width * 2
    low = lax.broadcasted_iota(jnp.int32, (half, 128), 1) < CB
    row2 = lax.broadcasted_iota(jnp.int32, (half, 128), 0)
    cols, thirds = [], []
    for kx in range(3):
        for ky in range(3):
            start = base2 + ky - 1 - (step if kx == 0 else 0)
            a, b = [hid[0 if kx == 1 else 1, h, pl.ds(start, half, stride=2), :] for h in range(2)]
            if ky == 0:
                a = jnp.where(row2 % 2 == 0, 0.0, a)
                b = jnp.where(row2 % 2 == 0, 0.0, b)
            ra = pltpu.roll(a, 64, 1)
            rb = pltpu.roll(b, 64, 1)
            pair_k = [jnp.where(low, 0.0, ra), jnp.where(low, ra, rb)]
            cols.append(jnp.concatenate(pair_k, axis=0).astype(BF16))
            thirds.append((a, b) if len(thirds) % 2 else (ra, rb))
    thirds.append((0.0, 0.0))
    for p in range(5):
        pair_k = [jnp.where(low, f, l) for f, l in zip(thirds[2 * p], thirds[2 * p + 1])]
        cols.append(jnp.concatenate(pair_k, axis=0).astype(BF16))
    cols = jnp.concatenate(cols, axis=1)
    out = jnp.dot(cols, ordered[...], preferred_element_type=F32)
    up = jnp.concatenate([us[h, 0:half, :] for h in range(2)], axis=0)
    delta = leaky(out, up)
    delta_b = delta.astype(BF16)
    other = pltpu.roll(delta, 64, 1)
    low3 = lax.broadcasted_iota(jnp.int32, (2 * half, 128), 1) < CB
    turned = jnp.where(low3 == (section == 0), delta, other).astype(BF16)
    for two in range(7):
        grid = contract(cols[:, two * 256 : two * 256 + 256], turned, 0, 0)
        for tile in range(2):
            tap = 2 * two + tile
            if tap < 9:
                t2[pl.ds(tap * 192, 128), :] = grid[tile * 128 : tile * 128 + 128]
                continue
            for h in range(2):
                tap = 2 * (2 * two + tile - 9) + h
                if tap < 9:
                    row0 = tile * 128 + h * CB
                    t2[pl.ds(tap * 192 + 128, CB), :] = grid[row0 : row0 + CB]
    row3 = lax.broadcasted_iota(jnp.int32, (2 * half, 128), 0)
    next_y = row3 % 2 == 0
    next_x = row3 % half < half - 2 * width
    grid = contract(delta_b, ordered[...], 1, 1)
    grads = []
    for tap in range(9):
        c1 = grid[:, 1152 + tap // 2 * 128 : 1280 + tap // 2 * 128]
        c1 = c1 if tap % 2 else pltpu.roll(c1, 64, 1)
        grads.append([grid[:, tap * 128 : tap * 128 + 128], c1])

    def joined(late, early, distance, valid):
        return [
            l + jnp.where(valid, pltpu.roll(e, 2 * half - distance, 0), 0.0)
            for l, e in zip(late, early)
        ]

    for i in range(2):
        if i == 0:
            over_y = grads[3:6]
        else:
            over_y = [joined(grads[6 + ky], grads[ky], 2 * width, next_x) for ky in range(3)]
        for parity, (c0, c1) in enumerate((over_y[1], joined(over_y[2], over_y[0], 1, next_y))):
            turn = pltpu.roll(c0, 64, 1)
            k0, k1 = turn[:half], turn[half:]
            hgs[i, 0, pl.ds(parity, half, stride=2), :] = jnp.where(low, k0, c1[:half] + k1)
            hgs[i, 1, pl.ds(parity, half, stride=2), :] = jnp.where(low, k1, c1[half:])
    hidden_grad = jnp.concatenate(
        [
            jnp.concatenate(
                [hgs[n % 2, h, pl.ds(n // 2 * step, step), :] for n in range(2 * pairs)], axis=0
            )
            for h in range(2)
        ],
        axis=1,
    )
    hidden_grad = hidden_grad.astype(BF16).astype(F32)
    delta_a = leaky(hidden, hidden_grad)
    quarters = lax.broadcasted_iota(jnp.int32, (rows, 128), 1) // 32
    even, late = delta_a[:, :128], delta_a[:, 128:]
    even = jnp.where(section == 0, even, pltpu.roll(even, 96, 1))
    late = jnp.where(section == 0, pltpu.roll(late, 32, 1), late)
    delta_a = jnp.where(quarters % 2 == 0, even, late).astype(BF16)
    quarter = lax.broadcasted_iota(jnp.int32, (96, 128), 1) // 32
    for tap in range(9):
        grid = contract(columns[tap], delta_a, 0, 0)
        fold = jnp.concatenate([jnp.zeros((32, 128), F32), grid[0:64]], axis=0)
        for q, k in ((1, 2), (2, 1), (3, 3)):
            fold = jnp.where(quarter == q, grid[64 * k - 32 : 64 * k + 64], fold)
        fold = fold + pltpu.roll(fold, 64, 1)
        t1[pl.ds(tap * 96, 96), :] = fold + pltpu.roll(fold, 32, 1)
    r2, r1 = TAPS * CB // spread, TAPS * CA // spread
    h2, h1 = packed_rows(spread)
    t2[pl.ds(TAPS * CB, t2.shape[0] - TAPS * CB), :] = jnp.zeros((t2.shape[0] - TAPS * CB, 128), F32)
    t1[pl.ds(TAPS * CA, t1.shape[0] - TAPS * CA), :] = jnp.zeros((t1.shape[0] - TAPS * CA, 128), F32)
    low2 = lax.broadcasted_iota(jnp.int32, (h2, 128), 1) < CB
    quarter = lax.broadcasted_iota(jnp.int32, (h1, 128), 1) // 32
    upper = pair // (pairs // 2)

    def block(ref, n, stride, start, size):
        found = None
        for member in range(2):
            for x in range(2):
                d = 2 * (pairs - 1 - n if member else n) + x
                more = ref[pl.ds(d * stride + start, size), :]
                here = jnp.logical_and(upper == member, side == x)
                found = more if found is None else jnp.where(here, more, found)
        return found

    for n in range(pairs // 2):
        a = block(t2, n, r2, 0, h2)
        b = block(t2, n, r2, h2, h2)
        keep[n, 0:h2, :] = jnp.where(low2, a, b).astype(BF16)
        kept = block(t1, n, r1, 0, h1)
        for g in range(1, 4):
            kept = jnp.where(quarter == g, block(t1, n, r1, g * h1, h1), kept)
        keep[n, h2 : h2 + h1, :] = kept.astype(BF16)


def swap_order(pairs):
    return [*range(2, pairs)]


def packed_rows(spread):
    r2, r1 = TAPS * CB // spread, TAPS * CA // spread
    return round_up(-(-r2 // 2), 16), round_up(-(-r1 // 4), 16)


def unpack_body(spread, mine, got, first_out, second_out, first_buf, second_buf, sems):
    r2, r1 = TAPS * CB // spread, TAPS * CA // spread
    h2, h1 = packed_rows(spread)
    total = mine[...].astype(F32) + got[...].astype(F32)
    top = total[:h2].T
    second_buf[...] = jnp.concatenate([top[:CB], top[CB:]], axis=1)[:, :r2]
    second_copy = pltpu.make_async_copy(second_buf, second_out, sems.at[0])
    second_copy.start()
    rest = total[h2:].T
    rest = jnp.concatenate([rest[32 * g : 32 * g + 32] for g in range(4)], axis=1)
    first_buf[...] = rest[:, :r1]
    first_copy = pltpu.make_async_copy(first_buf, first_out, sems.at[1])
    first_copy.start()
    second_copy.wait()
    first_copy.wait()


def swap_bit(count, bit):
    return [(i, i ^ (1 << bit)) for i in range(count)]


def pick(array, index, axis):
    return lax.dynamic_index_in_dim(array, index, axis, keepdims=False)


def shards(input_field, first_weight, second_weight, upstream_grad):
    spread = lax.axis_size("space")
    pairs = spread // 2
    tail = pairs // 4
    pair = lax.axis_index("space") // 2

    hbm = pl.BlockSpec(memory_space=pltpu.HBM)
    pieces = pl.pallas_call(
        lambda *refs: cut_body(pairs, *refs),
        out_shape=[
            jax.ShapeDtypeStruct((2, 8 + (tail if k in (0, pairs - 1) else 0), 8, 256), BF16)
            for k in range(pairs)
        ]
        + [jax.ShapeDtypeStruct((8 + tail, 8, 256), BF16)],
        in_specs=[hbm, hbm],
        out_specs=[pl.BlockSpec(memory_space=pltpu.VMEM)] * (pairs + 1),
        scratch_shapes=[
            pltpu.VMEM(input_field.shape, BF16),
            pltpu.VMEM(upstream_grad.shape, BF16),
            pltpu.SemaphoreType.DMA((5,)),
        ],
        compiler_params=pltpu.CompilerParams(vmem_limit_bytes=16 << 20),
    )(
        pltpu.with_memory_space_constraint(input_field, pltpu.HBM),
        pltpu.with_memory_space_constraint(upstream_grad, pltpu.HBM),
    )
    mine = pieces[0]
    received = [None] * (pairs - 1)
    for k in range(1, pairs):
        route = [(2 * d + c, 2 * (d ^ (2 * k) ^ c) + c) for d in range(spread) for c in range(2)]
        received[k - 1] = lax.ppermute(pieces[k], ("space", "section"), route)
    partner = lax.ppermute(pieces[pairs], "space", swap_bit(spread, 0))
    banded, ordered = pl.pallas_call(
        weights_body,
        out_shape=[
            jax.ShapeDtypeStruct((9 * 256, 256), BF16),
            jax.ShapeDtypeStruct((14 * 128, 128), BF16),
        ],
        in_specs=[hbm, hbm],
        out_specs=[pl.BlockSpec(memory_space=pltpu.VMEM)] * 2,
        scratch_shapes=[
            pltpu.VMEM(first_weight.shape[::-1], BF16),
            pltpu.VMEM(second_weight.shape, BF16),
            pltpu.SemaphoreType.DMA((2,)),
        ],
        compiler_params=pltpu.CompilerParams(vmem_limit_bytes=16 << 20),
    )(
        pltpu.with_memory_space_constraint(first_weight.T, pltpu.HBM),
        pltpu.with_memory_space_constraint(second_weight, pltpu.HBM),
    )
    early = jnp.concatenate([received[k - 1].reshape(-1, 8, 256) for k in swap_order(pairs)])
    early = lax.ppermute(early, "section", swap_bit(2, 0))
    late, banded = lax.optimization_barrier((received[0].reshape(-1, 8, 256), banded))
    late = jnp.concatenate([late, partner])
    late = lax.ppermute(late, "section", swap_bit(2, 0))
    h2, h1 = packed_rows(spread)
    total = call(
        lambda *refs: main_body(pairs, spread, *refs),
        jax.ShapeDtypeStruct((pairs // 2, h2 + h1, 128), BF16),
        [
            pltpu.VMEM((2, 2, (2 * pairs + 1) * 64 + 16, 128), F32),
            pltpu.VMEM((2, 2, (pairs + 1) * 32 + 16, 128), F32),
            pltpu.VMEM((2, 2, pairs * 32 + 8, 128), F32),
            pltpu.VMEM((2, pairs * 16 + 16, 128), F32),
            pltpu.VMEM((TAPS * CB + 2 * h2, 128), F32),
            pltpu.VMEM((TAPS * CA + 4 * h1, 128), F32),
        ],
        (mine, partner, *received, early, late, banded, ordered),
    )

    def added(a, b):
        return (a.astype(F32) + b.astype(F32)).astype(BF16)

    bit = 0
    while total.shape[0] > 1:
        paired = total.reshape(total.shape[0] // 2, 2, *total.shape[1:])
        here = (group_of(pair, pairs) >> bit) & 1
        kept = pick(paired, here, 1)
        came = lax.ppermute(pick(paired, 1 - here, 1), "space", swap_bit(spread, bit + 1))
        total = added(kept, came)
        bit += 1
    total = total[0]
    replicas = lax.axis_size("dp")
    bit = 0
    while 1 << (bit + 1) < replicas:
        total = added(total, lax.ppermute(total, "dp", swap_bit(replicas, bit)))
        bit += 1
    came = lax.ppermute(total, "dp", swap_bit(replicas, bit))
    first_out = (CB // 2, TAPS * CA // spread)
    second_out = (CC // 2, TAPS * CB // spread)
    vmem = pl.BlockSpec(memory_space=pltpu.VMEM)
    first_grad, second_grad = pl.pallas_call(
        lambda *refs: unpack_body(spread, *refs),
        out_shape=[jax.ShapeDtypeStruct(first_out, F32), jax.ShapeDtypeStruct(second_out, F32)],
        in_specs=[vmem, vmem],
        out_specs=[hbm, hbm],
        scratch_shapes=[
            pltpu.VMEM(first_out, F32),
            pltpu.VMEM(second_out, F32),
            pltpu.SemaphoreType.DMA((2,)),
        ],
        compiler_params=pltpu.CompilerParams(vmem_limit_bytes=16 << 20),
    )(total, came)
    return (first_grad.T, second_grad.T)


def solution(mesh):
    return jax.shard_map(
        shards,
        mesh=mesh,
        in_specs=(
            P(None, "dp", "space", None, None, None),
            P(),
            P(),
            P(None, "dp", None, "space", None, None),
        ),
        out_specs=(P("space", "section"), P("space", "section")),
        check_vma=False,
    )
```

```python
import jax
import jax.numpy as jnp
from jax import lax
from jax.experimental import pallas as pl
from jax.experimental.pallas import tpu as pltpu
from jax.sharding import PartitionSpec as P

CA = 32
CB = 64
CC = 128
TAPS = 27
SLOPE = 0.3
BF16 = jnp.bfloat16
F32 = jnp.float32


def round_up(value, step):
    return -(-value // step) * step


def leaky(condition, value):
    return jnp.where(condition > 0, value, SLOPE * value)


def contract(a, b, dim_a, dim_b):
    return lax.dot_general(a, b, (((dim_a,), (dim_b,)), ((), ())), preferred_element_type=F32)


def call(body, out_shape, scratch, args):
    vmem = pl.BlockSpec(memory_space=pltpu.VMEM)
    many = isinstance(out_shape, (list, tuple))
    return pl.pallas_call(
        body,
        out_shape=out_shape,
        in_specs=[vmem] * len(args),
        out_specs=[vmem] * len(out_shape) if many else vmem,
        scratch_shapes=scratch,
        compiler_params=pltpu.CompilerParams(vmem_limit_bytes=32 << 20),
    )(*args)


def weights_body(weight_hbm, second_hbm, banded, ordered, weight, second, sems):
    copies = [
        pltpu.make_async_copy(weight_hbm, weight, sems.at[0]),
        pltpu.make_async_copy(second_hbm, second, sems.at[1]),
    ]
    for copy in copies:
        copy.start()
    for copy in copies:
        copy.wait()
    for tap in range(9):
        ordered[pl.ds(tap * 128, 128), :] = second[pl.ds(tap * 192, 128), :]
        ordered[pl.ds(1152 + tap * CB, CB), :] = second[pl.ds(tap * 192 + 128, CB), :]
    ordered[pl.ds(1152 + 9 * CB, CB), :] = jnp.zeros((CB, CC), BF16)
    lane = lax.broadcasted_iota(jnp.int32, (CA, 2 * CB), 1)
    zero = jnp.zeros((CA, 2 * CB), F32)
    turned = weight[...].astype(F32).T
    turned = jnp.concatenate([turned, turned], axis=1)
    for tap in range(9):
        left, right = [], []
        for kz in range(3):
            start = (3 * tap + kz) * CA
            both = turned[start : start + CA]
            left.append(jnp.where(lane < CB, both, 0.0))
            right.append(jnp.where(lane < CB, 0.0, both))
        for half in range(2):
            rows = []
            for z in range(8):
                block = zero
                for odd, side in ((0, left), (1, right)):
                    kz = z - 2 * (2 * half + odd) + 1
                    if 0 <= kz <= 2:
                        block = block + side[kz]
                rows.append(block)
            banded[pl.ds(tap * 256, 256), half * 128 : half * 128 + 128] = jnp.concatenate(
                rows, axis=0
            ).astype(BF16)


def group_of(pair, pairs):
    return jnp.minimum(pair, pairs - 1 - pair)


def cut_body(pairs, field_hbm, upstream_hbm, *refs):
    *outs, field, upstream, sems = refs
    pair = lax.axis_index("space") // 2
    copies = [
        pltpu.make_async_copy(field_hbm.at[m, 0, i], field.at[m, 0, i], sems.at[2 * m + i])
        for m in range(2)
        for i in range(2)
    ]
    copies.append(pltpu.make_async_copy(upstream_hbm, upstream, sems.at[4]))
    for copy in copies:
        copy.start()
    for copy in copies:
        copy.wait()

    def fill(out, k, micro):
        lower = group_of(pair ^ k, pairs)
        for i in range(2):
            for upper, member in enumerate((lower, pairs - 1 - lower)):
                out[pl.ds(4 * i + 2 * upper, 2)] = field[micro, 0, i, pl.ds(2 * member, 2)]
        if k in (0, pairs - 1):
            rows = [upstream[micro, 0, p, 0, pl.ds(j, 1), :] for j in range(2) for p in range(pairs)]
            rows = jnp.concatenate([r.astype(F32) for r in rows], axis=0).astype(BF16)
            out[pl.ds(8, pairs // 4)] = rows.reshape(pairs // 4, 8, 256)

    for k in range(pairs):
        for micro in range(2):
            fill(outs[k].at[micro], k, micro)
    outs[pairs][...] = outs[0][lax.axis_index("section")]


def main_body(pairs, spread, mine, partner, *refs):
    received = refs[: pairs - 1]
    early, late, banded, ordered, keep, xf, hid, hgs, us, t2, t1 = refs[pairs - 1 :]
    space = lax.axis_index("space")
    side, pair = space % 2, space // 2
    section = lax.axis_index("section")
    width = 8
    tail = pairs // 4
    base = width * 8 + 8
    total = 2 * pairs * width * 8
    for i in range(2):
        for h in range(2):
            xf[i, h, 0:base, :] = jnp.zeros((base, 128), F32)

    def place(load, k, at_side):
        there = pair ^ k
        start = pl.multiple_of(base + (2 * there + at_side) * (width * 8), 8)
        for micro in range(2):
            for i in range(2):
                tiles = load(micro, i * 4, 4).reshape(32, 256).astype(F32)
                for h in range(2):
                    xf[i, h, pl.ds(start + micro * 32, 32), :] = tiles[:, h * 128 : h * 128 + 128]
            if k in (0, pairs - 1):
                rows = load(micro, 8, tail).reshape(2 * pairs, 256).astype(F32)
                volume = 4 * micro + 2 * (there // (pairs // 2)) + at_side
                for j in range(2):
                    for h in range(2):
                        us[h, pl.ds(2 * volume + j, pairs, stride=2 * width), :] = rows[
                            j * pairs : j * pairs + pairs, h * 128 : h * 128 + 128
                        ]

    place(lambda micro, at, size: mine[micro, pl.ds(at, size)], 0, side)
    last = 2 * received[0].shape[1]
    place(
        lambda micro, at, size: jnp.where(
            section == micro, partner[pl.ds(at, size)], late[pl.ds(last + at, size)]
        ),
        0,
        1 - side,
    )
    offset = 0
    for k in [1] + swap_order(pairs):
        ref = received[k - 1]
        place(lambda micro, at, size: ref[micro, pl.ds(at, size)], k, side ^ section)
        swapped = late if k == 1 else early
        start = 0 if k == 1 else offset
        place(
            lambda micro, at, size: swapped[pl.ds(start + micro * ref.shape[1] + at, size)],
            k,
            1 - (side ^ section),
        )
        offset += 0 if k == 1 else 2 * ref.shape[1]

    rows = total // 2
    row = lax.broadcasted_iota(jnp.int32, (rows, 256), 0)
    columns = []
    for kx in range(3):
        for ky in range(3):
            start = base + ky - 1 - (width * 8 if kx == 0 else 0)
            part = jnp.concatenate(
                [xf[0 if kx == 1 else 1, h, pl.ds(start, rows, stride=2), :] for h in range(2)],
                axis=1,
            )
            if ky == 0:
                part = jnp.where(row % 4 == 0, 0.0, part)
            columns.append(part.astype(BF16))
    preact = jnp.dot(jnp.concatenate(columns, axis=1), banded[...], preferred_element_type=F32)
    hidden = leaky(preact, preact).astype(BF16).astype(F32)
    step = width * 4
    base2 = step + 8
    for i in range(2):
        picked = jnp.concatenate(
            [hidden[(2 * n + i) * step : (2 * n + i + 1) * step] for n in range(pairs)], axis=0
        )
        for h in range(2):
            hid[i, h, 0:base2, :] = jnp.zeros((base2, 128), F32)
            hid[i, h, pl.ds(base2, pairs * step), :] = picked[:, h * 128 : h * 128 + 128]
    half = pairs * width * 2
    low = lax.broadcasted_iota(jnp.int32, (half, 128), 1) < CB
    row2 = lax.broadcasted_iota(jnp.int32, (half, 128), 0)
    cols, thirds = [], []
    for kx in range(3):
        for ky in range(3):
            start = base2 + ky - 1 - (step if kx == 0 else 0)
            a, b = [hid[0 if kx == 1 else 1, h, pl.ds(start, half, stride=2), :] for h in range(2)]
            if ky == 0:
                a = jnp.where(row2 % 2 == 0, 0.0, a)
                b = jnp.where(row2 % 2 == 0, 0.0, b)
            ra = pltpu.roll(a, 64, 1)
            rb = pltpu.roll(b, 64, 1)
            pair_k = [jnp.where(low, 0.0, ra), jnp.where(low, ra, rb)]
            cols.append(jnp.concatenate(pair_k, axis=0).astype(BF16))
            thirds.append((a, b) if len(thirds) % 2 else (ra, rb))
    thirds.append((0.0, 0.0))
    for p in range(5):
        pair_k = [jnp.where(low, f, l) for f, l in zip(thirds[2 * p], thirds[2 * p + 1])]
        cols.append(jnp.concatenate(pair_k, axis=0).astype(BF16))
    cols = jnp.concatenate(cols, axis=1)
    out = jnp.dot(cols, ordered[...], preferred_element_type=F32)
    up = jnp.concatenate([us[h, 0:half, :] for h in range(2)], axis=0)
    delta = leaky(out, up)
    delta_b = delta.astype(BF16)
    other = pltpu.roll(delta, 64, 1)
    low3 = lax.broadcasted_iota(jnp.int32, (2 * half, 128), 1) < CB
    turned = jnp.where(low3 == (section == 0), delta, other).astype(BF16)
    for two in range(7):
        grid = contract(cols[:, two * 256 : two * 256 + 256], turned, 0, 0)
        for tile in range(2):
            tap = 2 * two + tile
            if tap < 9:
                t2[pl.ds(tap * 192, 128), :] = grid[tile * 128 : tile * 128 + 128]
                continue
            for h in range(2):
                tap = 2 * (2 * two + tile - 9) + h
                if tap < 9:
                    row0 = tile * 128 + h * CB
                    t2[pl.ds(tap * 192 + 128, CB), :] = grid[row0 : row0 + CB]
    row3 = lax.broadcasted_iota(jnp.int32, (2 * half, 128), 0)
    next_y = row3 % 2 == 0
    gap = jnp.zeros((2 * width, 128), F32)
    grid = contract(delta_b, ordered[...], 1, 1)
    grads = []
    for tap in range(9):
        c1 = grid[:, 1152 + tap // 2 * 128 : 1280 + tap // 2 * 128]
        c1 = c1 if tap % 2 else pltpu.roll(c1, 64, 1)
        grads.append([grid[:, tap * 128 : tap * 128 + 128], c1])

    def next_cell(late, early):
        moved = [jnp.where(next_y, pltpu.roll(e, 2 * half - 1, 0), 0.0) for e in early]
        return [l + e for l, e in zip(late, moved)]

    def next_plane(late, early):
        moved = [
            jnp.concatenate([e[2 * width : half], gap, e[half + 2 * width :], gap], axis=0)
            for e in early
        ]
        return [l + e for l, e in zip(late, moved)]

    for i in range(2):
        if i == 0:
            over_y = grads[3:6]
        else:
            over_y = [next_plane(grads[6 + ky], grads[ky]) for ky in range(3)]
        for parity, (c0, c1) in enumerate((over_y[1], next_cell(over_y[2], over_y[0]))):
            turn = pltpu.roll(c0, 64, 1)
            k0, k1 = turn[:half], turn[half:]
            hgs[i, 0, pl.ds(parity, half, stride=2), :] = jnp.where(low, k0, c1[:half] + k1)
            hgs[i, 1, pl.ds(parity, half, stride=2), :] = jnp.where(low, k1, c1[half:])
    hidden_grad = jnp.concatenate(
        [
            jnp.concatenate(
                [hgs[n % 2, h, pl.ds(n // 2 * step, step), :] for n in range(2 * pairs)], axis=0
            )
            for h in range(2)
        ],
        axis=1,
    )
    hidden_grad = hidden_grad.astype(BF16).astype(F32)
    delta_a = leaky(hidden, hidden_grad)
    quarters = lax.broadcasted_iota(jnp.int32, (rows, 128), 1) // 32
    even, late = delta_a[:, :128], delta_a[:, 128:]
    even = jnp.where(section == 0, even, pltpu.roll(even, 96, 1))
    late = jnp.where(section == 0, pltpu.roll(late, 32, 1), late)
    delta_a = jnp.where(quarters % 2 == 0, even, late).astype(BF16)
    quarter = lax.broadcasted_iota(jnp.int32, (96, 128), 1) // 32
    for tap in range(9):
        grid = contract(columns[tap], delta_a, 0, 0)
        fold = jnp.concatenate([jnp.zeros((32, 128), F32), grid[0:64]], axis=0)
        for q, k in ((1, 2), (2, 1), (3, 3)):
            fold = jnp.where(quarter == q, grid[64 * k - 32 : 64 * k + 64], fold)
        fold = fold + pltpu.roll(fold, 64, 1)
        t1[pl.ds(tap * 96, 96), :] = fold + pltpu.roll(fold, 32, 1)
    r2, r1 = TAPS * CB // spread, TAPS * CA // spread
    h2, h1 = packed_rows(spread)
    t2[pl.ds(TAPS * CB, t2.shape[0] - TAPS * CB), :] = jnp.zeros((t2.shape[0] - TAPS * CB, 128), F32)
    t1[pl.ds(TAPS * CA, t1.shape[0] - TAPS * CA), :] = jnp.zeros((t1.shape[0] - TAPS * CA, 128), F32)
    low2 = lax.broadcasted_iota(jnp.int32, (h2, 128), 1) < CB
    quarter = lax.broadcasted_iota(jnp.int32, (h1, 128), 1) // 32
    upper = pair // (pairs // 2)

    def block(ref, n, stride, start, size):
        found = None
        for member in range(2):
            for x in range(2):
                d = 2 * (pairs - 1 - n if member else n) + x
                more = ref[pl.ds(d * stride + start, size), :]
                here = jnp.logical_and(upper == member, side == x)
                found = more if found is None else jnp.where(here, more, found)
        return found

    for n in range(pairs // 2):
        a = block(t2, n, r2, 0, h2)
        b = block(t2, n, r2, h2, h2)
        keep[n, 0:h2, :] = jnp.where(low2, a, b).astype(BF16)
        kept = block(t1, n, r1, 0, h1)
        for g in range(1, 4):
            kept = jnp.where(quarter == g, block(t1, n, r1, g * h1, h1), kept)
        keep[n, h2 : h2 + h1, :] = kept.astype(BF16)


def swap_order(pairs):
    return [*range(2, pairs)]


def packed_rows(spread):
    r2, r1 = TAPS * CB // spread, TAPS * CA // spread
    return round_up(-(-r2 // 2), 16), round_up(-(-r1 // 4), 16)


def unpack_body(spread, mine, got, first_out, second_out, first_buf, second_buf, sems):
    r2, r1 = TAPS * CB // spread, TAPS * CA // spread
    h2, h1 = packed_rows(spread)
    total = mine[...].astype(F32) + got[...].astype(F32)
    top = total[:h2].T
    copies = []
    for part in range(2):
        rows = pl.ds(part * (CB // 2), CB // 2)
        upper = top[part * (CB // 2) : (part + 1) * (CB // 2)]
        lower = top[CB + part * (CB // 2) : CB + (part + 1) * (CB // 2)]
        second_buf[rows, :] = jnp.concatenate([upper, lower], axis=1)[:, :r2]
        copies.append(pltpu.make_async_copy(second_buf.at[rows], second_out.at[rows], sems.at[part]))
        copies[-1].start()
    rest = total[h2:].T
    rest = jnp.concatenate([rest[32 * g : 32 * g + 32] for g in range(4)], axis=1)
    first_buf[...] = rest[:, :r1]
    copies.append(pltpu.make_async_copy(first_buf, first_out, sems.at[2]))
    copies[-1].start()
    for copy in copies:
        copy.wait()


def swap_bit(count, bit):
    return [(i, i ^ (1 << bit)) for i in range(count)]


def pick(array, index, axis):
    return lax.dynamic_index_in_dim(array, index, axis, keepdims=False)


def shards(input_field, first_weight, second_weight, upstream_grad):
    spread = lax.axis_size("space")
    pairs = spread // 2
    tail = pairs // 4
    pair = lax.axis_index("space") // 2

    hbm = pl.BlockSpec(memory_space=pltpu.HBM)
    pieces = pl.pallas_call(
        lambda *refs: cut_body(pairs, *refs),
        out_shape=[
            jax.ShapeDtypeStruct((2, 8 + (tail if k in (0, pairs - 1) else 0), 8, 256), BF16)
            for k in range(pairs)
        ]
        + [jax.ShapeDtypeStruct((8 + tail, 8, 256), BF16)],
        in_specs=[hbm, hbm],
        out_specs=[pl.BlockSpec(memory_space=pltpu.VMEM)] * (pairs + 1),
        scratch_shapes=[
            pltpu.VMEM(input_field.shape, BF16),
            pltpu.VMEM(upstream_grad.shape, BF16),
            pltpu.SemaphoreType.DMA((5,)),
        ],
        compiler_params=pltpu.CompilerParams(vmem_limit_bytes=16 << 20),
    )(
        pltpu.with_memory_space_constraint(input_field, pltpu.HBM),
        pltpu.with_memory_space_constraint(upstream_grad, pltpu.HBM),
    )
    mine = pieces[0]
    received = [None] * (pairs - 1)
    for k in range(1, pairs):
        route = [(2 * d + c, 2 * (d ^ (2 * k) ^ c) + c) for d in range(spread) for c in range(2)]
        received[k - 1] = lax.ppermute(pieces[k], ("space", "section"), route)
    partner = lax.ppermute(pieces[pairs], "space", swap_bit(spread, 0))
    banded, ordered = pl.pallas_call(
        weights_body,
        out_shape=[
            jax.ShapeDtypeStruct((9 * 256, 256), BF16),
            jax.ShapeDtypeStruct((14 * 128, 128), BF16),
        ],
        in_specs=[hbm, hbm],
        out_specs=[pl.BlockSpec(memory_space=pltpu.VMEM)] * 2,
        scratch_shapes=[
            pltpu.VMEM(first_weight.shape[::-1], BF16),
            pltpu.VMEM(second_weight.shape, BF16),
            pltpu.SemaphoreType.DMA((2,)),
        ],
        compiler_params=pltpu.CompilerParams(vmem_limit_bytes=16 << 20),
    )(
        pltpu.with_memory_space_constraint(first_weight.T, pltpu.HBM),
        pltpu.with_memory_space_constraint(second_weight, pltpu.HBM),
    )
    early = jnp.concatenate([received[k - 1].reshape(-1, 8, 256) for k in swap_order(pairs)])
    early = lax.ppermute(early, "section", swap_bit(2, 0))
    late, banded = lax.optimization_barrier((received[0].reshape(-1, 8, 256), banded))
    late = jnp.concatenate([late, partner])
    late = lax.ppermute(late, "section", swap_bit(2, 0))
    h2, h1 = packed_rows(spread)
    total = call(
        lambda *refs: main_body(pairs, spread, *refs),
        jax.ShapeDtypeStruct((pairs // 2, h2 + h1, 128), BF16),
        [
            pltpu.VMEM((2, 2, (2 * pairs + 1) * 64 + 16, 128), F32),
            pltpu.VMEM((2, 2, (pairs + 1) * 32 + 16, 128), F32),
            pltpu.VMEM((2, 2, pairs * 32 + 8, 128), F32),
            pltpu.VMEM((2, pairs * 16 + 16, 128), F32),
            pltpu.VMEM((TAPS * CB + 2 * h2, 128), F32),
            pltpu.VMEM((TAPS * CA + 4 * h1, 128), F32),
        ],
        (mine, partner, *received, early, late, banded, ordered),
    )

    def added(a, b):
        return (a.astype(F32) + b.astype(F32)).astype(BF16)

    bit = 0
    while total.shape[0] > 1:
        paired = total.reshape(total.shape[0] // 2, 2, *total.shape[1:])
        here = (group_of(pair, pairs) >> bit) & 1
        kept = pick(paired, here, 1)
        came = lax.ppermute(pick(paired, 1 - here, 1), "space", swap_bit(spread, bit + 1))
        total = added(kept, came)
        bit += 1
    total = total[0]
    replicas = lax.axis_size("dp")
    bit = 0
    while 1 << (bit + 1) < replicas:
        total = added(total, lax.ppermute(total, "dp", swap_bit(replicas, bit)))
        bit += 1
    came = lax.ppermute(total, "dp", swap_bit(replicas, bit))
    first_out = (CB // 2, TAPS * CA // spread)
    second_out = (CC // 2, TAPS * CB // spread)
    vmem = pl.BlockSpec(memory_space=pltpu.VMEM)
    first_grad, second_grad = pl.pallas_call(
        lambda *refs: unpack_body(spread, *refs),
        out_shape=[jax.ShapeDtypeStruct(first_out, F32), jax.ShapeDtypeStruct(second_out, F32)],
        in_specs=[vmem, vmem],
        out_specs=[hbm, hbm],
        scratch_shapes=[
            pltpu.VMEM(first_out, F32),
            pltpu.VMEM(second_out, F32),
            pltpu.SemaphoreType.DMA((3,)),
        ],
        compiler_params=pltpu.CompilerParams(vmem_limit_bytes=16 << 20),
    )(total, came)
    return (first_grad.T, second_grad.T)


def solution(mesh):
    return jax.shard_map(
        shards,
        mesh=mesh,
        in_specs=(
            P(None, "dp", "space", None, None, None),
            P(),
            P(),
            P(None, "dp", None, "space", None, None),
        ),
        out_specs=(P("space", "section"), P("space", "section")),
        check_vma=False,
    )
```
